32 devices in a mesh: tm: 2 (over x), lat: 4 (over y, core), lon: 4 (over z).
Axes of the slice: x: 2, y: 2, z: 4, core: 2. Of those that a mesh axis runs over, the one named last changes fastest.
Arguments:
- control: float32 [16, 8, 64, 512], P(None, None, 'lat', 'lon'), may hold values from -6 to 6
- ens_pert: bfloat16 [2, 16, 8, 64, 512], P('tm', None, None, 'lat', 'lon'), may hold values from -6 to 6
- lat_filter: bfloat16 [64, 64], replicated, may hold values from 0 to 2.5, as said below
- lon_filter: bfloat16 [512, 512], replicated, may hold values from 0 to 2.5, as said below
- interp_lat: float32 [128, 18], P('lat'), may hold values from -1.5 to 1.5
- interp_lon: float32 [1024, 130], P('lon'), may hold values from -0.5 to 0.5
- obs_cell: int32 [2, 2, 4, 4, 64], P('tm', None, 'lat', 'lon'), may hold values from 0 to 65535
- obs_count: int32 [2, 2, 4, 4], P('tm', None, 'lat', 'lon'), may hold values from 1 to 64, as said below
- obs_value: float32 [2, 2, 4, 4, 64], P('tm', None, 'lat', 'lon'), may hold values from -18 to 18
- obs_weight: float32 [2, 2, 4, 4, 64], P('tm', None, 'lat', 'lon'), may hold values from 0.1 to 0.4
Outputs:
- gradient: float32 [16, 8, 64, 512], P(None, None, 'lat', 'lon')
The draws below stay inside these ranges and needn't reach their ends.
Inputs may be any that keep to these rules, and one draw needn't show every extreme that they name: `lat_filter`: within the latitude spreading matrix all entries are non-negative. `lon_filter`: entries are non-negative. `obs_count`: each count is at least 1 and at most 64; in every draw some count equals 64.
All inputs are finite; a program needn't handle non-finite values.
Results may differ from the reference program's by a relative error of at most 0.0003.
Values sent between devices are 32-bit elements; how exact they have to be, the bound alone decides.
No kernel may reach another device: no remote copies, remote signals or barrier semaphores. Data moves between devices by JAX's collectives and lax.ppermute only.
A program may use at most 64 MiB of HBM per device.

```python
import math
import jax
import jax.numpy as jnp
from jax import lax

MEM = 16
LEV = 8
CLAT = 16
CLON = 128
CAP = 64
SLOTS = 2
NLAT = 64
NLON = 512
FLAT = 32
FLON = 256
N_TM = 2
N_LAT = 4
N_LON = 4


def filter_table(key, length, reach, periodic):
    places = jnp.arange(length)
    distance = jnp.abs(places[:, None] - places[None, :]).astype(jnp.float32)
    if periodic:
        distance = jnp.minimum(distance, length - distance)
    factor = jax.random.uniform(key, (length, length), jnp.float32, 0.5, 1.5)
    table = jnp.exp(-distance / reach) * factor / jnp.sqrt(jnp.float32(reach))
    table = table + 0.5 * jnp.eye(length, dtype=jnp.float32)
    return table.astype(jnp.bfloat16)


def draw_lat_filter(key, part):
    return filter_table(jax.random.fold_in(key, 11), NLAT, 2.0 * CLAT, False)


def draw_lon_filter(key, part):
    return filter_table(jax.random.fold_in(key, 23), NLON, 2.0 * CLON, True)


def draw_obs_count(key, part):
    first, second, third = jax.random.split(jax.random.fold_in(key, 37), 3)
    shape = (N_TM, SLOTS, N_LAT, N_LON)
    level = jax.random.randint(first, (1, SLOTS, 1, 1), 1, 5)
    upper = 1 + CAP * level // 4
    counts = jax.random.randint(second, shape, 1, upper + 1)
    counts = jnp.minimum(counts, CAP)
    choose = jax.random.randint(third, (), 0, N_TM * SLOTS * N_LAT * N_LON)
    counts = counts.reshape(-1).at[choose].set(CAP).reshape(shape)
    return counts.astype(jnp.int32)


def with_ends(entries, own_key, smallest, high):
    longest = entries.shape.index(max(entries.shape))
    spots = []
    for shift in (0, 1):
        where = [jax.random.randint(jax.random.fold_in(own_key, axis), (), 0, length) for axis, length in enumerate(entries.shape)]
        where[longest] = (where[longest] + shift) % entries.shape[longest]
        spots.append(tuple(where))
    return entries.at[spots[0]].set(smallest).at[spots[1]].set(high)


def level_of(key, dims, cuts, smallest, high):
    def one(position, parts):
        steps = jax.random.uniform(jax.random.fold_in(jax.random.fold_in(key, 6), position), (parts,), jnp.float32, smallest / len(cuts), high / len(cuts))
        return jnp.repeat(jnp.exp(steps), dims[position] // parts).reshape((-1,) + (1,) * (len(dims) - position - 1))

    loudness = one(*cuts[0])
    for cut in cuts[1:]:
        loudness = loudness * one(*cut)
    return loudness


def bell_draw(rng, shape, width, most, cuts=(), kind=jnp.bfloat16):
    drawn = jax.random.normal(rng, shape, jnp.float32) * width
    if len(cuts) > 0:
        drawn = level_of(rng, shape, cuts, -0.22, 0.18) * drawn
    return jnp.clip(drawn, min=-most, max=most).astype(kind)


def setup_inputs(seed: int = 0) -> dict:
    streams_of = jax.random.split(jax.random.key(seed), 11)
    return {
        "control": bell_draw(streams_of[0], (MEM, LEV, NLAT, NLON), 1.0, 6.0, ((2, 4), (3, 4)), jnp.float32),
        "ens_pert": bell_draw(streams_of[1], (SLOTS, MEM, LEV, NLAT, NLON), 1.0, 6.0, ((0, 2), (3, 4), (4, 4))),
        "lat_filter": draw_lat_filter(jax.random.fold_in(streams_of[10], 71), 0),
        "lon_filter": draw_lon_filter(jax.random.fold_in(streams_of[10], 71), 0),
        "interp_lat": bell_draw(streams_of[4], (N_LAT * FLAT, CLAT + 2), (CLAT + 2) ** -0.5, 1.5, ((0, 4),), jnp.float32),
        "interp_lon": bell_draw(streams_of[5], (N_LON * FLON, CLON + 2), (CLON + 2) ** -0.5, 0.5, ((0, 4),), jnp.float32),
        "obs_cell": with_ends(jax.random.randint(streams_of[6], (N_TM, SLOTS, N_LAT, N_LON, CAP), 0, LEV * FLAT * FLON), jax.random.fold_in(streams_of[6], 1), 0, (LEV * FLAT * FLON) - 1).astype(jnp.int32),
        "obs_count": draw_obs_count(jax.random.fold_in(streams_of[10], 71), 0),
        "obs_value": bell_draw(streams_of[8], (N_TM, SLOTS, N_LAT, N_LON, CAP), 3.0, 18.0, ((0, 2), (2, 4), (3, 4)), jnp.float32),
        "obs_weight": jnp.clip(jnp.exp(math.log(0.4) - 1.3862944 * jax.random.uniform(streams_of[9], (N_TM, SLOTS, N_LAT, N_LON, CAP), jnp.float32) ** level_of(streams_of[9], (N_TM, SLOTS, N_LAT, N_LON, CAP), ((0, 2), (2, 4), (3, 4)), -0.2, 0.2)), 0.1, 0.4),
    }


HIGHEST = lax.Precision.HIGHEST

def spread_both(source, lat_matrix, lon_matrix):
    across = jnp.einsum('ab,mlbc->mlac', lat_matrix, source, precision=HIGHEST)
    return jnp.einsum('mlac,dc->mlad', across, lon_matrix, precision=HIGHEST)

def to_fine(increment, interp_lat, interp_lon):
    padded = jnp.pad(increment, ((0, 0), (1, 1), (0, 0)))
    padded = jnp.concatenate([padded[:, :, -1:], padded, padded[:, :, :1]], axis=2)
    lat_index = (jnp.arange(N_LAT)[:, None] * CLAT + jnp.arange(CLAT + 2)[None, :]).astype(jnp.int32)
    lon_index = (jnp.arange(N_LON)[:, None] * CLON + jnp.arange(CLON + 2)[None, :]).astype(jnp.int32)
    windows = padded[:, lat_index][:, :, :, lon_index]
    lat_blocks = interp_lat.reshape(N_LAT, FLAT, CLAT + 2)
    lon_blocks = interp_lon.reshape(N_LON, FLON, CLON + 2)
    rowwise = jnp.einsum('aip,lapbq->abliq', lat_blocks, windows, precision=HIGHEST)
    result = jnp.einsum('abliq,bjq->ablij', rowwise, lon_blocks, precision=HIGHEST)
    return result.reshape(N_LAT, N_LON, LEV * FLAT * FLON)

def reference(control, ens_pert, lat_filter, lon_filter, interp_lat, interp_lon, obs_cell, obs_count, obs_value, obs_weight):
    lat_matrix = lat_filter.astype(jnp.float32)
    lon_matrix = lon_filter.astype(jnp.float32)
    slot_range = jnp.arange(CAP).astype(jnp.int32)
    usable = (slot_range[None, None, None, None, :] < obs_count[..., None]).astype(jnp.float32)

    def arrange(table):
        return jnp.transpose(table, (1, 2, 3, 0, 4)).reshape(SLOTS, N_LAT, N_LON, N_TM * CAP)
    columns = arrange(obs_cell)
    targets = arrange(obs_value)
    weights = arrange(obs_weight * usable)

    def observe(source):
        spread = spread_both(source, lat_matrix, lon_matrix)

        def one_slot(inputs):
            members, places = inputs
            increment = lax.optimization_barrier(jnp.sum(spread * members.astype(jnp.float32), axis=0))
            finer = to_fine(increment, interp_lat, interp_lon)
            return jnp.take_along_axis(finer, places, axis=2)
        return lax.map(one_slot, (ens_pert, columns))
    values, pullback = jax.vjp(observe, control)
    departure = weights * (values - targets)
    adjoint, = pullback(departure)
    return control + adjoint
```

```python
import functools

import jax
import jax.numpy as jnp
from jax import lax
from jax.experimental import pallas as pl
from jax.experimental.pallas import tpu as pltpu
from jax.sharding import PartitionSpec as P

HIGHEST = lax.Precision.HIGHEST
F32 = jnp.float32
BF16 = jnp.bfloat16


def swap(x, axis, k):
    n = lax.axis_size(axis)
    return lax.ppermute(x, axis, [(i, i ^ k) for i in range(n)])


def two_pass(x, w, dims):
    high = x.astype(BF16)
    low = (x - high.astype(F32)).astype(BF16)
    dot = functools.partial(
        lax.dot_general, dimension_numbers=dims, preferred_element_type=F32
    )
    return dot(high, w) + dot(low, w)


def vmem_call(kernel, out_shape, flops, nbytes, scratch=(), smem=0, total=0):
    specs = [pl.BlockSpec(memory_space=pltpu.SMEM)] * smem
    specs += [pl.BlockSpec(memory_space=pltpu.VMEM)] * (total - smem)
    return pl.pallas_call(
        kernel,
        out_shape=out_shape,
        in_specs=specs,
        out_specs=jax.tree.map(lambda _: pl.BlockSpec(memory_space=pltpu.VMEM), out_shape),
        scratch_shapes=list(scratch),
        cost_estimate=pl.CostEstimate(flops=flops, bytes_accessed=nbytes, transcendentals=0),
    )


def increment_kernel(bands, slots, *refs):
    fields = refs[:bands]
    table = refs[bands]
    pert = refs[bands + 1 : bands + 1 + slots * bands]
    outs = refs[bands + 1 + slots * bands :]
    width = fields[0].shape[1]
    rows = outs[0].shape[0]
    shares = fields[0].shape[0] // rows
    source = jnp.concatenate([f[...] for f in fields], axis=1)
    spread = two_pass(source, table[...], (((1,), (1,)), ((), ())))
    for q in range(slots):
        for k in range(bands):
            total = None
            for m in range(shares):
                part = spread[m * rows : (m + 1) * rows, k * width : (k + 1) * width]
                part = part * pert[q * bands + k][m * rows : (m + 1) * rows, :].astype(F32)
                total = part if total is None else total + part
            outs[q][:, k * width : (k + 1) * width] = total


def adjoint_kernel(bands, slots, *refs):
    grads = refs[:slots]
    table = refs[slots]
    pert = refs[slots + 1 : slots + 1 + slots * bands]
    outs = refs[slots + 1 + slots * bands :]
    width = outs[0].shape[1]
    rows = grads[0].shape[0]
    shares = outs[0].shape[0] // rows
    columns = []
    for k in range(bands):
        pieces = []
        for m in range(shares):
            total = None
            for q in range(slots):
                part = grads[q][:, k * width : (k + 1) * width]
                part = part * pert[q * bands + k][m * rows : (m + 1) * rows, :].astype(F32)
                total = part if total is None else total + part
            pieces.append(total)
        columns.append(jnp.concatenate(pieces, axis=0))
    source = jnp.concatenate(columns, axis=1)
    result = two_pass(source, table[...], (((1,), (0,)), ((), ())))
    for k in range(bands):
        outs[k][...] = result[:, k * width : (k + 1) * width]


def observe_kernel(bands, levels, rows, padded, width, *refs):
    places = refs[0]
    inc, low, high = refs[1:4]
    lists = refs[4 : 4 + bands]
    out, window, grad = refs[4 + bands :]
    filler = jnp.zeros((padded - rows - 2, width), F32)
    for k in range(bands):
        span = slice(k * width, (k + 1) * width)
        for level in range(levels):
            block = [
                inc[level * rows : (level + 1) * rows, span],
                low[level : level + 1, span],
                high[level : level + 1, span],
                filler,
            ]
            window[k, level * padded : (level + 1) * padded, :] = jnp.concatenate(block, axis=0)
    grad[...] = jnp.zeros_like(grad)
    lane = lax.broadcasted_iota(jnp.int32, (levels * padded, width), 1)
    first = places[2 * bands].astype(F32)
    for k in range(bands):
        before, after = places[k], places[bands + k]
        main = lists[k][:width, :]
        rowpart = lists[k][width : width + padded, :]
        tail = width + padded
        left = lists[k][tail : tail + 1, :]
        right = lists[k][tail + 1 : tail + 2, :]
        level_of = lists[k][tail + 2 : tail + 3, :]
        value = lists[k][tail + 3 : tail + 4, :]
        weight = lists[k][tail + 4 : tail + 5, :]
        seen_by = lax.dot_general(
            window[k], main, (((1,), (0,)), ((), ())),
            precision=HIGHEST, preferred_element_type=F32,
        )
        seen_by += window[before][:, width - 1 : width] * left
        seen_by += window[after][:, 0:1] * right
        chosen = jnp.concatenate(
            [jnp.where(level_of == first + level, rowpart, 0.0) for level in range(levels)], axis=0
        )
        seen = jnp.sum(chosen * seen_by, axis=0, keepdims=True)
        weighted = chosen * (weight * (seen - value))
        grad[k] += lax.dot_general(
            weighted, main, (((1,), (1,)), ((), ())),
            precision=HIGHEST, preferred_element_type=F32,
        )
        onto_left = jnp.sum(weighted * left, axis=1, keepdims=True)
        onto_right = jnp.sum(weighted * right, axis=1, keepdims=True)
        grad[before] += jnp.where(lane == width - 1, onto_left, 0.0)
        grad[after] += jnp.where(lane == 0, onto_right, 0.0)
    for k in range(bands):
        out[:, k * width : (k + 1) * width] = grad[k]


def per_device(
    control,
    ens_pert,
    lat_filter,
    lon_filter,
    interp_lat,
    interp_lon,
    obs_cell,
    obs_count,
    obs_value,
    obs_weight,
):
    slots, lats, lons = (lax.axis_size(axis) for axis in ("tm", "lat", "lon"))
    t, a, b = (lax.axis_index(axis) for axis in ("tm", "lat", "lon"))
    members, levels, rows, width = control.shape
    share = members // slots
    group = levels // lons
    fields = share * group * rows
    fine_rows, fine_cols = interp_lat.shape[0], interp_lon.shape[0]
    padded = -(-(rows + 2) // 8) * 8
    slot_pert = ens_pert[0]

    slot_range = jnp.arange(obs_cell.shape[-1])
    usable = (slot_range < obs_count[0, :, 0, 0, None]).astype(F32)
    held = jnp.stack(
        [
            obs_cell[0, :, 0, 0].astype(F32),
            obs_value[0, :, 0, 0],
            obs_weight[0, :, 0, 0] * usable,
        ],
        axis=1,
    )
    own_lists = [lax.dynamic_index_in_dim(held, t, 0, False)]
    for q in range(1, slots):
        own_lists.append(swap(lax.dynamic_index_in_dim(held, t ^ q, 0, False), "tm", q))
    package = jnp.concatenate(own_lists, axis=1)
    cells = package[0].astype(jnp.int32)
    level_of = cells // (fine_rows * fine_cols)
    row_of = (cells // fine_cols) % fine_rows
    col_of = cells % fine_cols
    row_hot = (jnp.arange(fine_rows)[:, None] == row_of[None, :]).astype(F32)
    col_hot = (jnp.arange(fine_cols)[:, None] == col_of[None, :]).astype(F32)
    row_part = jnp.einsum("ip,io->po", interp_lat, row_hot, precision=HIGHEST)
    col_part = jnp.einsum("jq,jo->qo", interp_lon, col_hot, precision=HIGHEST)
    blank = functools.partial(jnp.zeros, dtype=F32)
    count = cells.shape[0]
    listing = jnp.concatenate(
        [
            col_part[1 : width + 1],
            row_part[1 : rows + 1],
            row_part[:1],
            row_part[rows + 1 :],
            blank((padded - rows - 2, count)),
            col_part[:1],
            col_part[width + 1 :],
            level_of.astype(F32)[None],
            package[1:3],
            blank((3, count)),
        ],
        axis=0,
    )

    def level_slice(x, k):
        return lax.dynamic_slice_in_dim(x, (b ^ k) * group, group, 1)

    def member_slice(x, q):
        return lax.dynamic_slice_in_dim(x, (t ^ q) * share, share, 0)

    def to_group(x):
        pieces = [level_slice(x, 0).astype(F32)]
        for k in range(1, lons):
            pieces.append(swap(level_slice(x, k).astype(F32), "lon", k))
        return [p.reshape(fields, width) for p in pieces]

    crossing = [swap(member_slice(slot_pert, q).astype(F32), "tm", q) for q in range(1, slots)]
    pert = to_group(member_slice(slot_pert, 0))
    for x in crossing:
        pert += to_group(x)

    lat_matrix = lat_filter.astype(F32)

    def lat_block(i, j):
        return lax.dynamic_slice(lat_matrix, (i * rows, j * rows), (rows, rows))

    def lat_mix(x, block):
        other = swap(x, "lat", 1)
        total = None
        for h in range(0, lats, 2):
            part = jnp.einsum("ab,mbk->mak", block(a ^ h, a), x, precision=HIGHEST)
            part += jnp.einsum("ab,mbk->mak", block(a ^ h, a ^ 1), other, precision=HIGHEST)
            total = part if h == 0 else total + swap(part, "lat", h)
        return total

    mine = member_slice(control, 0).reshape(share * levels, rows, width)
    mixed = lat_mix(mine, lat_block).reshape(share, levels, rows, width)
    source = to_group(mixed)

    listings = [listing] + [swap(listing, "lon", k) for k in range(1, lons)]

    tall = jnp.concatenate(
        [lax.dynamic_slice_in_dim(lon_filter, (b ^ k) * width, width, 0) for k in range(lons)], axis=0
    )
    table = jnp.concatenate(
        [lax.dynamic_slice_in_dim(tall, (b ^ k) * width, width, 1) for k in range(lons)], axis=1
    )
    whole = lons * width
    lines = group * rows
    flops = 4 * fields * whole * whole
    nbytes = 4 * fields * whole * (1 + slots) + 2 * whole * whole + 4 * slots * lines * whole
    partial = vmem_call(
        functools.partial(increment_kernel, lons, slots),
        [jax.ShapeDtypeStruct((lines, whole), F32)] * slots,
        flops,
        nbytes,
        total=lons + 1 + slots * lons,
    )(*source, table, *pert)
    increment = partial[0]
    for q in range(1, slots):
        increment = increment + swap(partial[q], "tm", q)

    up = [(i, i + 1) for i in range(lats - 1)]
    down = [(i + 1, i) for i in range(lats - 1)]
    by_level = increment.reshape(group, rows, whole)
    low = lax.ppermute(by_level[:, rows - 1], "lat", up)
    high = lax.ppermute(by_level[:, 0], "lat", down)
    order = jnp.arange(lons)
    band = b ^ order
    places = jnp.concatenate([b ^ ((band - 1) % lons), b ^ ((band + 1) % lons), (b * group)[None]])
    tall_rows = group * padded
    grad_pad = vmem_call(
        functools.partial(observe_kernel, lons, group, rows, padded, width),
        jax.ShapeDtypeStruct((tall_rows, whole), F32),
        24 * tall_rows * whole * count,
        4 * whole * (lines + tall_rows) + 4 * lons * listing.size,
        scratch=[pltpu.VMEM((lons, tall_rows, width), F32)] * 2,
        smem=1,
        total=4 + lons,
    )(places.astype(jnp.int32), increment, low, high, *listings)
    grad_pad = grad_pad.reshape(group, padded, whole)
    to_last = lax.ppermute(grad_pad[:, rows], "lat", down)
    to_first = lax.ppermute(grad_pad[:, rows + 1], "lat", up)
    coarse = jnp.concatenate(
        [
            grad_pad[:, :1] + to_first[:, None],
            grad_pad[:, 1 : rows - 1],
            grad_pad[:, rows - 1 : rows] + to_last[:, None],
        ],
        axis=1,
    ).reshape(lines, whole)
    coarses = [coarse] + [swap(coarse, "tm", q) for q in range(1, slots)]

    pieces = vmem_call(
        functools.partial(adjoint_kernel, lons, slots),
        [jax.ShapeDtypeStruct((fields, width), F32)] * lons,
        flops,
        nbytes,
        total=slots + 1 + slots * lons,
    )(*coarses, table, *pert)
    shape = (share, group, rows, width)
    pieces = [pieces[0]] + [swap(pieces[k], "lon", k) for k in range(1, lons)]

    def lat_block_t(i, j):
        return lat_block(j, i).T

    result = control
    step = max(lons // 2, 1)
    for start in range(0, lons, step):
        some = jnp.stack(pieces[start : start + step]).reshape(step * share * group, rows, width)
        some = lat_mix(some, lat_block_t)
        for q in range(slots):
            arrived = some if q == 0 else swap(some, "tm", q)
            arrived = arrived.reshape((step,) + shape)
            for k in range(step):
                at = ((t ^ q) * share, (b ^ (start + k)) * group, 0, 0)
                old = lax.dynamic_slice(control, at, shape)
                result = lax.dynamic_update_slice(result, old + arrived[k], at)
    return result


def solution(mesh):
    placed = (
        P(None, None, "lat", "lon"),
        P("tm", None, None, "lat", "lon"),
        P(),
        P(),
        P("lat", None),
        P("lon", None),
        P("tm", None, "lat", "lon", None),
        P("tm", None, "lat", "lon"),
        P("tm", None, "lat", "lon", None),
        P("tm", None, "lat", "lon", None),
    )
    return jax.shard_map(
        per_device,
        mesh=mesh,
        in_specs=placed,
        out_specs=P(None, None, "lat", "lon"),
        check_vma=False,
    )
```

```python
import functools
import math

import jax
import jax.numpy as jnp
from jax import lax
from jax.experimental import pallas as pl
from jax.experimental.pallas import tpu as pltpu
from jax.sharding import PartitionSpec as P

HIGHEST = lax.Precision.HIGHEST
F32 = jnp.float32
BF16 = jnp.bfloat16


def swap(x, axis, k):
    n = lax.axis_size(axis)
    return lax.ppermute(x, axis, [(i, i ^ k) for i in range(n)])


def split(x):
    high = x.astype(BF16)
    return high, (x - high.astype(F32)).astype(BF16)


def dot(x, y, dims=((1,), (0,)), precision=None):
    return lax.dot_general(
        x, y, (dims, ((), ())), precision=precision, preferred_element_type=F32
    )


def vmem_call(kernel, out_shape, operands, flops, scratch=(), smem=0):
    specs = [pl.BlockSpec(memory_space=pltpu.SMEM)] * smem
    specs += [pl.BlockSpec(memory_space=pltpu.VMEM)] * (len(operands) - smem)
    nbytes = sum(math.prod(x.shape) * x.dtype.itemsize for x in [*operands, *out_shape])
    return pl.pallas_call(
        kernel,
        out_shape=out_shape,
        in_specs=specs,
        out_specs=[pl.BlockSpec(memory_space=pltpu.VMEM)] * len(out_shape),
        scratch_shapes=list(scratch),
        cost_estimate=pl.CostEstimate(flops=flops, bytes_accessed=nbytes, transcendentals=0),
    )(*operands)


def struct(*shape):
    return jax.ShapeDtypeStruct(shape, F32)


def lat_kernel(own, other, weights, *outs):
    size = weights.shape[1] // 2
    count = own.shape[0] // size
    columns = [
        jnp.concatenate([ref[i * size : (i + 1) * size, :] for ref in (own, other)], axis=0)
        for i in range(count)
    ]
    high, low = split(jnp.concatenate(columns, axis=1))
    width = own.shape[1]
    table = weights[...]
    result = dot(table, high) + dot(table, low)
    for h, out in enumerate(outs):
        for i in range(count):
            out[i * size : (i + 1) * size, :] = result[
                h * size : (h + 1) * size, i * width : (i + 1) * width
            ]


def increment_kernel(bands, slots, edges, rows, *refs):
    fields, table = refs[:bands], refs[bands]
    pert = refs[bands + 1 : bands + 1 + slots * bands]
    out = refs[bands + 1 + slots * bands]
    width = fields[0].shape[1]
    lines = out.shape[1]
    shares = fields[0].shape[0] // lines
    spread = 0.0
    for k in range(bands):
        high, low = split(fields[k][...])
        part = table[k * width : (k + 1) * width, :]
        spread += dot(high, part) + dot(low, part)
    for q in range(slots):
        for k in range(bands):
            span = slice(k * width, (k + 1) * width)
            total = None
            for m in range(shares):
                part = spread[m * lines : (m + 1) * lines, span]
                part = part * pert[q * bands + k][m * lines : (m + 1) * lines, :]
                total = part if total is None else total + part
            out[q, :, span] = total
            if edges:
                first, last = refs[-2:]
                for level in range(lines // rows):
                    at = q * (lines // rows) + level
                    first[at : at + 1, span] = total[level * rows : level * rows + 1]
                    last[at : at + 1, span] = total[(level + 1) * rows - 1 : (level + 1) * rows]


def adjoint_kernel(bands, slots, rows, *refs):
    coarse, table = refs[: 3 * slots], refs[3 * slots]
    pert = refs[3 * slots + 1 : 3 * slots + 1 + slots * bands]
    outs = refs[3 * slots + 1 + slots * bands :]
    width = outs[0].shape[1]
    lines = coarse[0].shape[0]
    shares = outs[0].shape[0] // lines
    grads = []
    for q in range(slots):
        core, first, last = coarse[3 * q : 3 * q + 3]
        line = lax.broadcasted_iota(jnp.int32, (rows, bands * width), 0)
        parts = []
        for level in range(lines // rows):
            part = core[level * rows : (level + 1) * rows, :]
            part += jnp.where(line == 0, first[level : level + 1, :], 0.0)
            part += jnp.where(line == rows - 1, last[level : level + 1, :], 0.0)
            parts.append(part)
        grads.append(parts[0] if len(parts) == 1 else jnp.concatenate(parts, axis=0))
    result = 0.0
    for k in range(bands):
        span = slice(k * width, (k + 1) * width)
        pieces = []
        for m in range(shares):
            total = None
            for q in range(slots):
                part = grads[q][:, span] * pert[q * bands + k][m * lines : (m + 1) * lines, :]
                total = part if total is None else total + part
            pieces.append(total)
        high, low = split(jnp.concatenate(pieces, axis=0))
        part = table[span, :]
        result += dot(high, part) + dot(low, part)
    for k in range(bands):
        outs[k][...] = result[:, k * width : (k + 1) * width]


def observe_kernel(bands, held, levels, rows, padded, width, *refs):
    places, inc, low, high = refs[:4]
    lists = refs[4 : 4 + held]
    core, to_last, to_first, window, grad = refs[4 + held :]
    filler = jnp.zeros((padded - rows - 2, width), F32)
    lane = lax.broadcasted_iota(jnp.int32, (levels * padded, width), 1)
    first = places[2 * bands].astype(F32)
    grad[...] = jnp.zeros_like(grad)
    for j in range(held):
        for k in range(bands):
            span = slice(k * width, (k + 1) * width)
            for level in range(levels):
                at = j * levels + level
                block = [
                    inc[j, level * rows : (level + 1) * rows, span],
                    low[at : at + 1, span],
                    high[at : at + 1, span],
                    filler,
                ]
                window[j * bands + k, level * padded : (level + 1) * padded, :] = (
                    jnp.concatenate(block, axis=0)
                )
    tail = width + padded
    for j in range(held):
        for k in range(bands):
            before = j * bands + places[k]
            after = j * bands + places[bands + k]
            main = lists[j][k, :width, :]
            rowpart = lists[j][k, width:tail, :]
            ends = lists[j][k, tail : tail + 8, :]
            left, right = ends[0:1], ends[1:2]
            seen_by = dot(window[j * bands + k], main, precision=HIGHEST)
            seen_by += window[before][:, width - 1 : width] * left
            seen_by += window[after][:, 0:1] * right
            chosen = jnp.concatenate(
                [
                    jnp.where(ends[2:3] == first + level, rowpart, 0.0)
                    for level in range(levels)
                ],
                axis=0,
            )
            seen = jnp.sum(chosen * seen_by, axis=0, keepdims=True)
            weighted = chosen * (ends[4:5] * (seen - ends[3:4]))
            grad[j * bands + k] += dot(weighted, main, ((1,), (1,)), precision=HIGHEST)
            onto_left = jnp.sum(weighted * left, axis=1, keepdims=True)
            onto_right = jnp.sum(weighted * right, axis=1, keepdims=True)
            grad[before] += jnp.where(lane == width - 1, onto_left, 0.0)
            grad[after] += jnp.where(lane == 0, onto_right, 0.0)
    for j in range(held):
        for k in range(bands):
            span = slice(k * width, (k + 1) * width)
            done = grad[j * bands + k]
            for level in range(levels):
                at = j * levels + level
                base = level * padded
                core[j, level * rows : (level + 1) * rows, span] = done[base : base + rows]
                to_last[at : at + 1, span] = done[base + rows : base + rows + 1]
                to_first[at : at + 1, span] = done[base + rows + 1 : base + rows + 2]


def per_device(
    control,
    ens_pert,
    lat_filter,
    lon_filter,
    interp_lat,
    interp_lon,
    obs_cell,
    obs_count,
    obs_value,
    obs_weight,
):
    slots, lats, lons = (lax.axis_size(axis) for axis in ("tm", "lat", "lon"))
    t, a, b = (lax.axis_index(axis) for axis in ("tm", "lat", "lon"))
    members, levels, rows, width = control.shape
    held = math.gcd(slots, levels // lons)
    parts = slots // held
    share = members // parts
    group = levels // (lons * held)
    lines = group * rows
    fields = share * lines
    whole = lons * width
    fine_rows, fine_cols = interp_lat.shape[0], interp_lon.shape[0]
    padded = -(-(rows + 2) // 8) * 8

    def part_of(x, q):
        owner = t ^ q
        x = x.reshape(members, lons, held, group, rows, width)
        at = (owner // held * share, 0, owner % held, 0, 0, 0)
        x = lax.dynamic_slice(x, at, (share, lons, 1, group, rows, width))
        return x.reshape(share, lons, group, rows, width)

    def to_group(x):
        pieces = []
        for k in range(lons):
            piece = lax.dynamic_index_in_dim(x, b ^ k, 1, False).astype(F32)
            pieces.append(piece.reshape(fields, width))
        return pieces[:1] + [swap(pieces[k], "lon", k) for k in range(1, lons)]

    def lat_block(i, j):
        return lax.dynamic_slice(lat_filter, (i * rows, j * rows), (rows, rows))

    def lat_weights(count, back):
        repeat = math.gcd(count, max(128 // rows, 1))
        eye = jnp.eye(repeat, dtype=BF16)
        tall = []
        for h in range(0, lats, 2):
            wide = []
            for j in (0, 1):
                block = lat_block(a ^ j, a ^ h).T if back else lat_block(a ^ h, a ^ j)
                wide.append((eye[:, None, :, None] * block[None, :, None, :]).reshape(
                    repeat * rows, repeat * rows
                ))
            tall.append(jnp.concatenate(wide, axis=1))
        return jnp.concatenate(tall, axis=0)

    def lat_mix(x, weights):
        other = swap(x, "lat", 1)
        flops = 4 * weights.shape[0] * 2 * x.size
        out = vmem_call(lat_kernel, [struct(*x.shape)] * (lats // 2), [x, other, weights], flops)
        return out[0], [swap(out[h], "lat", 2 * h) for h in range(1, lats // 2)]

    slot_pert = ens_pert[0]
    mine = part_of(control, 0).reshape(share * lons * group * rows, width)
    kept, arrived = lat_mix(mine, lat_weights(share * lons * group, False))
    crossing = [swap(part_of(slot_pert, q).astype(F32), "tm", q) for q in range(1, slots)]
    pert = to_group(part_of(slot_pert, 0))

    slot_range = jnp.arange(obs_cell.shape[-1])
    usable = (slot_range < obs_count[0, :, 0, 0, None]).astype(F32)
    package = jnp.stack(
        [
            obs_cell[0, :, 0, 0].astype(F32),
            obs_value[0, :, 0, 0],
            obs_weight[0, :, 0, 0] * usable,
        ],
        axis=1,
    )
    own_lists = [lax.dynamic_index_in_dim(package, t, 0, False)]
    for q in range(1, slots):
        own_lists.append(swap(lax.dynamic_index_in_dim(package, t ^ q, 0, False), "tm", q))
    package = jnp.concatenate(own_lists, axis=1)
    cells = package[0].astype(jnp.int32)
    level_of = cells // (fine_rows * fine_cols)
    row_of = (cells // fine_cols) % fine_rows
    col_of = cells % fine_cols
    row_hot = (jnp.arange(fine_rows)[:, None] == row_of[None, :]).astype(F32)
    col_hot = (jnp.arange(fine_cols)[:, None] == col_of[None, :]).astype(F32)
    row_part = jnp.einsum("ip,io->po", interp_lat, row_hot, precision=HIGHEST)
    col_part = jnp.einsum("jq,jo->qo", interp_lon, col_hot, precision=HIGHEST)
    blank = functools.partial(jnp.zeros, dtype=F32)
    count = cells.shape[0]
    listing = jnp.concatenate(
        [
            col_part[1 : width + 1],
            row_part[1 : rows + 1],
            row_part[:1],
            row_part[rows + 1 :],
            blank((padded - rows - 2, count)),
            col_part[:1],
            col_part[width + 1 :],
            level_of.astype(F32)[None],
            package[1:3],
            blank((3, count)),
        ],
        axis=0,
    )
    near = jnp.stack([listing] + [swap(listing, "lon", k) for k in range(1, lons)])
    listings = [near] + [swap(near, "tm", j) for j in range(1, held)]

    for x in crossing:
        pert += to_group(x)
    for x in arrived:
        kept = kept + x
    source = to_group(kept.reshape(share, lons, group, rows, width))

    tall = jnp.concatenate(
        [lax.dynamic_slice_in_dim(lon_filter, (b ^ k) * width, width, 0) for k in range(lons)], axis=0
    )
    table = jnp.concatenate(
        [lax.dynamic_slice_in_dim(tall, (b ^ k) * width, width, 1) for k in range(lons)], axis=1
    )
    flops = 4 * fields * whole * whole
    edges = parts == 1
    shapes = [struct(slots, lines, whole)] + [struct(held * group, whole)] * (2 * edges)
    increment, *ends = vmem_call(
        functools.partial(increment_kernel, lons, slots, edges, rows),
        shapes,
        [*source, table.T, *pert],
        flops,
    )
    if not edges:
        total = increment[:held]
        for h in range(held, slots, held):
            total = total + swap(increment[h : h + held], "tm", h)
        increment = total
        by_level = total.reshape(held * group, rows, whole)
        ends = [by_level[:, 0], by_level[:, rows - 1]]

    up = [(i, i + 1) for i in range(lats - 1)]
    down = [(i + 1, i) for i in range(lats - 1)]
    high = lax.ppermute(ends[0], "lat", down)
    low = lax.ppermute(ends[1], "lat", up)
    band = b ^ jnp.arange(lons)
    start = (b * held + t % held) * group
    places = jnp.concatenate([b ^ ((band - 1) % lons), b ^ ((band + 1) % lons), start[None]])
    tall_rows = group * padded
    core, to_last, to_first = vmem_call(
        functools.partial(observe_kernel, lons, held, group, rows, padded, width),
        [struct(held, lines, whole)] + [struct(held * group, whole)] * 2,
        [places.astype(jnp.int32), increment, low, high, *listings],
        24 * held * tall_rows * whole * count,
        scratch=[pltpu.VMEM((held * lons, tall_rows, width), F32)] * 2,
        smem=1,
    )
    sent = [core, lax.ppermute(to_first, "lat", up), lax.ppermute(to_last, "lat", down)]
    coarse = []
    for h in range(0, slots, held):
        here = sent if h == 0 else [swap(x, "tm", h) for x in sent]
        for j in range(held):
            coarse += [here[0][j]] + [x[j * group : (j + 1) * group] for x in here[1:]]

    pieces = vmem_call(
        functools.partial(adjoint_kernel, lons, slots, rows),
        [struct(fields, width)] * lons,
        [*coarse, table, *pert],
        flops,
    )
    pieces = [pieces[0]] + [swap(pieces[k], "lon", k) for k in range(1, lons)]
    step = max(lons // 2, 1)
    weights = lat_weights(step * share * group, True)
    shape = (share, 1, 1, group, rows, width)
    by_group = control.reshape(members, lons, held, group, rows, width)
    result = by_group
    for first in range(0, lons, step):
        some = jnp.concatenate(pieces[first : first + step], axis=0)
        some, arrived = lat_mix(some, weights)
        for x in arrived:
            some = some + x
        for q in range(slots):
            here = some if q == 0 else swap(some, "tm", q)
            here = here.reshape((step,) + shape)
            owner = t ^ q
            for k in range(step):
                at = (owner // held * share, b ^ (first + k), owner % held, 0, 0, 0)
                old = lax.dynamic_slice(by_group, at, shape)
                result = lax.dynamic_update_slice(result, old + here[k], at)
    return result.reshape(control.shape)


def solution(mesh):
    placed = (
        P(None, None, "lat", "lon"),
        P("tm", None, None, "lat", "lon"),
        P(),
        P(),
        P("lat", None),
        P("lon", None),
        P("tm", None, "lat", "lon", None),
        P("tm", None, "lat", "lon"),
        P("tm", None, "lat", "lon", None),
        P("tm", None, "lat", "lon", None),
    )
    return jax.shard_map(
        per_device,
        mesh=mesh,
        in_specs=placed,
        out_specs=P(None, None, "lat", "lon"),
        check_vma=False,
    )
```

```python
import functools
import math

import jax
import jax.numpy as jnp
from jax import lax
from jax.experimental import pallas as pl
from jax.experimental.pallas import tpu as pltpu
from jax.sharding import PartitionSpec as P

HIGHEST = lax.Precision.HIGHEST
F32 = jnp.float32
BF16 = jnp.bfloat16


def swap(x, axis, k):
    n = lax.axis_size(axis)
    return lax.ppermute(x, axis, [(i, i ^ k) for i in range(n)])


def split(x):
    high = x.astype(BF16)
    return high, (x - high.astype(F32)).astype(BF16)


def dot(x, y, dims=((1,), (0,)), precision=None):
    return lax.dot_general(
        x, y, (dims, ((), ())), precision=precision, preferred_element_type=F32
    )


def vmem_call(kernel, out_shape, operands, flops, scratch=(), smem=0):
    specs = [pl.BlockSpec(memory_space=pltpu.SMEM)] * smem
    specs += [pl.BlockSpec(memory_space=pltpu.VMEM)] * (len(operands) - smem)
    nbytes = sum(math.prod(x.shape) * x.dtype.itemsize for x in [*operands, *out_shape])
    return pl.pallas_call(
        kernel,
        out_shape=out_shape,
        in_specs=specs,
        out_specs=[pl.BlockSpec(memory_space=pltpu.VMEM)] * len(out_shape),
        scratch_shapes=list(scratch),
        cost_estimate=pl.CostEstimate(flops=flops, bytes_accessed=nbytes, transcendentals=0),
    )(*operands)


def struct(*shape):
    return jax.ShapeDtypeStruct(shape, F32)


def cut_kernel(bands, slots, share, group, *refs):
    pert, outs, first, last = refs[0], refs[1:-2], refs[-2], refs[-1]
    rows, width = pert.shape[4:]
    t, b = lax.axis_index("tm"), lax.axis_index("lon")
    held = pert.shape[2]
    for q in range(slots):
        member = lax.div(t ^ q, held) * share
        level = lax.rem(t ^ q, held)
        for k in range(bands):
            for inner in range(group):
                part = pert[pl.ds(member, share), b ^ k, level, inner]
                part = part.astype(F32)
                at = inner * share * rows
                outs[q * bands + k][at : at + share * rows, :] = part.reshape(share * rows, width)
                at = ((q * bands + k) * group + inner) * share
                first[at : at + share, :] = part[:, 0, :]
                last[at : at + share, :] = part[:, rows - 1, :]


def weight_kernel(lats, rows, repeat, matrix, ahead, back):
    a = lax.axis_index("lat")
    length = matrix.shape[1]
    size = repeat * rows
    full = size + 2 * repeat
    iota = lax.broadcasted_iota

    def pick(shape, axis, wanted):
        return jnp.where(iota(jnp.int32, shape, axis) == wanted, 1.0, 0.0).astype(BF16)

    def block(to, of):
        line = iota(jnp.int32, (full, length), 0)
        rim = line - size
        wanted = jnp.where(
            rim < 0,
            to * rows + jnp.bitwise_and(line, rows - 1),
            to * rows + jnp.where(rim < repeat, -1, rows),
        )
        chosen = dot(pick((full, length), 1, wanted), matrix[...]).astype(BF16)
        column = iota(jnp.int32, (length, size), 1)
        chosen = dot(chosen, pick((length, size), 0, of * rows + jnp.bitwise_and(column, rows - 1)))
        line, column = iota(jnp.int32, (full, size), 0), iota(jnp.int32, (full, size), 1)
        rim = line - size
        field = jnp.where(rim < 0, line // rows, jnp.bitwise_and(rim, repeat - 1))
        return jnp.where(field == column // rows, chosen, 0.0)

    for h in range(0, lats, 2):
        at = h // 2 * full
        wide = jnp.concatenate([block(a ^ h, a ^ j) for j in (0, 1)], axis=1)
        ahead[at : at + full, :] = jnp.concatenate([wide, wide], axis=1).astype(BF16)
        at = h // 2 * size
        wide = jnp.concatenate([block(a ^ j, a ^ h).T for j in (0, 1)], axis=1)
        back[at : at + size, :] = jnp.concatenate([wide, wide], axis=1).astype(BF16)


def package_kernel(slots, count, cell, value, weight, *outs):
    t = lax.axis_index("tm")
    cap = cell.shape[1]
    entry = lax.broadcasted_iota(jnp.int32, (1, cap), 1)
    for q in range(slots):
        slot = t ^ q
        at = pl.ds(slot, 1)
        usable = jnp.where(entry < count[slot], 1.0, 0.0)
        lines = [cell[at, :].astype(F32), value[at, :], weight[at, :] * usable]
        outs[q][...] = jnp.concatenate(lines + [jnp.zeros((5, cap), F32)], axis=0)


def list_kernel(bands, slots, width, rows, padded, fuse, *refs):
    package, interp_lat, interp_lon = refs[:slots], refs[slots], refs[slots + 1]
    rims, (listing, edges, *outs) = refs[slots + 2 : 2 * slots + 2], refs[2 * slots + 2 :]
    fine_rows, fine_cols = interp_lat.shape[0], interp_lon.shape[0]
    cap = package[0].shape[1]
    for h in range(slots):
        lines = package[h][...]
        cell = lines[0:1] + 0.5
        level = jnp.floor(cell * (1.0 / (fine_rows * fine_cols)))
        inside = cell - level * (fine_rows * fine_cols)
        row = jnp.floor(inside * (1.0 / fine_cols))
        col = jnp.floor(inside - row * fine_cols)

        def picked(table, index):
            line = lax.broadcasted_iota(jnp.int32, (table.shape[0], cap), 0)
            hot = jnp.where(line == index.astype(jnp.int32), 1.0, 0.0)
            return dot(table[...], hot, ((0,), (0,)), precision=HIGHEST)

        by_col, by_row = picked(interp_lon, col), picked(interp_lat, row)
        last = [by_col[:1], by_col[width + 1 : width + 2], level, lines[1:3], lines[3:6]]
        part = jnp.concatenate(
            [
                by_col[1 : width + 1],
                by_row[1 : rows + 1],
                by_row[:1],
                by_row[rows + 1 : rows + 2],
                jnp.zeros((padded - rows - 2, cap), F32),
                *last,
            ],
            axis=0,
        )
        for out in [listing, *outs] if fuse else [listing]:
            out[: part.shape[0], h * cap : (h + 1) * cap] = part
    for k, out in enumerate([edges, *outs]):
        count = rims[0].shape[1]
        at = out.shape[0] - slots * count
        for q in range(slots):
            out[at + q * count : at + (q + 1) * count, :] = rims[q][k]


def gather_kernel(*refs):
    out = refs[-1]
    for k, ref in enumerate(refs[:-1]):
        out[k] = ref[: out.shape[1], :]


def pairs(blocks):
    return [
        blocks[i] if i + 1 == len(blocks) else jnp.concatenate(blocks[i : i + 2], axis=1)
        for i in range(0, len(blocks), 2)
    ]


def lat_kernel(bands, share, group, rows, repeat, own, other, weights, *outs):
    table = weights[...]
    size, width = repeat * rows, own.shape[1]
    full = size + 2 * repeat
    fields = group * share * rows
    tall = fields + 2 * group * share
    blocks = []
    for i in range(own.shape[0] // size):
        block = jnp.concatenate([ref[i * size : (i + 1) * size, :] for ref in (own, other)], axis=0)
        blocks.append(block)
    for pair, block in enumerate(pairs(blocks)):
        result = dot(table, jnp.concatenate(split(block), axis=0))
        for side in range(block.shape[1] // width):
            line = (2 * pair + side) * repeat
            band, inner, member = line // (group * share), line // share % group, line % share
            at = band * tall + (inner * share + member) * rows
            span = slice(side * width, (side + 1) * width)
            for h, out in enumerate(outs):
                base = h * full
                out[at : at + size, :] = result[base : base + size, span]
                for rim in (0, 1):
                    to = band * tall + fields + (2 * inner + rim) * share + member
                    of = base + size + rim * repeat
                    out[to : to + repeat, :] = result[of : of + repeat, span]


def lat_back_kernel(bands, share, group, rows, repeat, own, other, weights, *outs):
    table = weights[...]
    size, width = repeat * rows, own.shape[1]
    fields = group * share * rows
    tall = fields + 2 * group * share
    blocks, where = [], []
    for k in range(bands):
        for inner in range(group):
            for member in range(0, share, repeat):
                block = []
                for ref in (own, other):
                    at = k * tall + (inner * share + member) * rows
                    block.append(ref[at : at + size, :])
                    for rim in (0, 1):
                        at = k * tall + fields + (2 * inner + rim) * share + member
                        block.append(ref[at : at + repeat, :])
                blocks.append(jnp.concatenate(block, axis=0))
                where.append((k, (inner * share + member) * rows))
    for pair, block in enumerate(pairs(blocks)):
        result = dot(table, jnp.concatenate(split(block), axis=0))
        for side in range(block.shape[1] // width):
            k, at = where[2 * pair + side]
            span = slice(side * width, (side + 1) * width)
            for h in range(len(outs) // bands):
                outs[h * bands + k][at : at + size, :] = result[h * size : (h + 1) * size, span]


def increment_stage(sizes, source, table, pert, rims, window):
    bands, slots, share, group, rows, padded, width = sizes
    fields = group * share * rows
    pieces = [split(f[...]) for f in source]
    high, low = (jnp.concatenate([p[i] for p in pieces], axis=1) for i in (0, 1))
    part = table[...]
    spread = dot(high, part) + dot(low, part)
    filler = jnp.zeros((padded - rows - 2, width), F32)
    for q in range(slots):
        for k in range(bands):
            span = slice(k * width, (k + 1) * width)
            for inner in range(group):
                total = None
                for m in range(share):
                    at = (inner * share + m) * rows
                    term = spread[at : at + rows, span] * pert[q * bands + k][at : at + rows, :]
                    total = term if total is None else total + term
                block = [total]
                for rim in (0, 1):
                    at = (2 * inner + rim) * share
                    at_edge = rims[k].shape[0] + (q - slots) * 2 * group * share + at
                    edge = rims[k][at_edge : at_edge + share, :]
                    edge = spread[fields + at : fields + at + share, span] * edge
                    block.append(jnp.sum(edge, axis=0, keepdims=True))
                at = (q * group + inner) * padded
                window[k, at : at + padded, :] = jnp.concatenate(block + [filler], axis=0)


def observe_stage(sizes, window, tables, grad):
    bands, _, _, _, _, _, width = sizes
    onto, back, chosen, ends = tables
    tall = chosen.shape[1]
    lane = lax.broadcasted_iota(jnp.int32, (tall, width), 1)
    b = lax.axis_index("lon")
    for k in range(bands):
        grad[k] = jnp.zeros((tall, width), F32)
    for k in range(bands):
        before = b ^ lax.rem((b ^ k) + bands - 1, bands)
        after = b ^ lax.rem((b ^ k) + 1, bands)
        upper, lower = split(window[k])
        table = onto[k]
        left, right = ends[k, 0:1], ends[k, 1:2]
        seen_by = dot(jnp.concatenate([upper, upper], axis=1), table) + dot(lower, table[:width])
        seen_by += window[before][:, width - 1 : width] * left
        seen_by += window[after][:, 0:1] * right
        pick = chosen[k]
        seen = jnp.sum(pick * seen_by, axis=0, keepdims=True)
        weighted = pick * (ends[k, 4:5] * (seen - ends[k, 3:4]))
        upper, lower = split(weighted)
        table = back[k]
        both = dot(upper, table)
        grad[k] += both[:, :width] + both[:, width:] + dot(lower, table[:, :width])
        onto_left = jnp.sum(weighted * left, axis=1, keepdims=True)
        onto_right = jnp.sum(weighted * right, axis=1, keepdims=True)
        grad[before] += jnp.where(lane == width - 1, onto_left, 0.0)
        grad[after] += jnp.where(lane == 0, onto_right, 0.0)


def adjoint_stage(sizes, grads, table, pert, rims, out):
    bands, slots, share, group, rows, padded, width = sizes
    held = slots // len(grads)
    fields = group * share * rows
    tall = fields + 2 * group * share
    columns = []
    for k in range(bands):
        pieces = []
        for inner in range(group):
            lines = [
                grads[q // held][k, pl.ds((q % held * group + inner) * padded, padded), :]
                for q in range(slots)
            ]
            for m in range(share):
                at = (inner * share + m) * rows
                pieces.append(sum(
                    lines[q][:rows] * pert[q * bands + k][at : at + rows, :] for q in range(slots)
                ))
        for inner in range(group):
            for rim in (0, 1):
                at = (2 * inner + rim) * share
                total = 0.0
                for q in range(slots):
                    line = (q % held * group + inner) * padded + rows + rim
                    line = grads[q // held][k, line : line + 1, :]
                    edge = rims[k].shape[0] + (q - slots) * 2 * group * share + at
                    total += line * rims[k][edge : edge + share, :]
                pieces.append(total)
        columns.append(split(jnp.concatenate(pieces, axis=0)))
    high, low = (jnp.concatenate([c[i] for c in columns], axis=1) for i in (0, 1))
    part = table[...]
    result = dot(high, part) + dot(low, part)
    for k in range(bands):
        out[k * tall : (k + 1) * tall, :] = result[:, k * width : (k + 1) * width]


def middle_kernel(sizes, *refs):
    bands, slots = sizes[:2]
    source, turned, table, rest = refs[:bands], refs[bands], refs[bands + 1], refs[bands + 2 :]
    pert, rims, rest = rest[: slots * bands], rest[slots * bands :][:bands], rest[(slots + 1) * bands :]
    tables, (out, window, grad) = rest[:4], rest[4:]
    increment_stage(sizes, source, turned, pert, rims, window)
    observe_stage(sizes, window, tables, grad)
    adjoint_stage(sizes, [grad], table, pert, rims, out)


def increment_kernel(sizes, *refs):
    bands = sizes[0]
    pert, out = refs[bands + 1 : -1], refs[-1]
    increment_stage(sizes, refs[:bands], refs[bands], pert, pert[sizes[1] * bands :], out)


def observe_kernel(sizes, window, onto, back, chosen, ends, grad):
    observe_stage(sizes, window, (onto, back, chosen, ends), grad)


def adjoint_kernel(sizes, sets, *refs):
    pert = refs[sets + 1 :]
    count = sizes[0] * sizes[1]
    adjoint_stage(sizes, refs[:sets], refs[sets], pert, pert[count:-1], pert[-1])


def prepare_kernel(bands, held, levels, padded, width, *refs):
    lists = refs[:held]
    onto, back, chosen, ends = refs[held:]
    count = lists[0].shape[2]
    first = (lax.axis_index("lon") * held + lax.rem(lax.axis_index("tm"), held)) * levels
    first = first.astype(F32)
    tail = width + padded
    for k in range(bands):
        for j in range(held):
            span = slice(j * count, (j + 1) * count)
            main = lists[j][k, :width, :]
            high, low = split(main)
            onto[k, :width, span] = high
            onto[k, width:, span] = low
            high, low = split(main.T)
            back[k, span, :width] = high
            back[k, span, width:] = low
            last = lists[j][k, tail : tail + 8, :]
            ends[k, :, span] = last
            rowpart = lists[j][k, width:tail, :]
            for other in range(held):
                for level in range(levels):
                    at = (other * levels + level) * padded
                    if other == j:
                        part = jnp.where(last[2:3] == first + level, rowpart, 0.0)
                    else:
                        part = jnp.zeros_like(rowpart)
                    chosen[k, at : at + padded, span] = part


def per_device(
    control,
    ens_pert,
    lat_filter,
    lon_filter,
    interp_lat,
    interp_lon,
    obs_cell,
    obs_count,
    obs_value,
    obs_weight,
):
    slots, lats, lons = (lax.axis_size(axis) for axis in ("tm", "lat", "lon"))
    t, a, b = (lax.axis_index(axis) for axis in ("tm", "lat", "lon"))
    members, levels, rows, width = control.shape
    held = math.gcd(slots, levels // lons)
    parts = slots // held
    share = members // parts
    group = levels // (lons * held)
    fields = group * share * rows
    edge = 2 * group * share
    tall = fields + edge
    whole = lons * width
    padded = -(-(rows + 2) // 8) * 8
    sizes = (lons, slots, share, group, rows, padded, width)
    split_up = (members, lons, held, group, rows, width)
    by_group = control.reshape(split_up)

    repeat = math.gcd(share, max(64 // rows, 1))

    size = repeat * rows
    full = size + 2 * repeat
    ahead, weights = vmem_call(
        functools.partial(weight_kernel, lats, rows, repeat),
        [
            jax.ShapeDtypeStruct((lats // 2 * full, 4 * size), BF16),
            jax.ShapeDtypeStruct((lats // 2 * size, 4 * full), BF16),
        ],
        [lat_filter],
        0,
    )

    count = slots * lons
    cut = vmem_call(
        functools.partial(cut_kernel, lons, slots, share, group),
        [struct(fields, width)] * count + [struct(count * group * share, width)] * 2,
        [ens_pert[0].reshape(split_up)],
        0,
    )
    pert = [None] * count
    order = [*range(2, lons), *range(1, min(lons, 2)), 0]
    for k in order:
        for q in range(slots):
            piece = cut[q * lons + k]
            if q > 0:
                piece = swap(piece, "tm", q)
            pert[q * lons + k] = piece if k == 0 else swap(piece, "lon", k)
    up = [(i, i + 1) for i in range(lats - 1)]
    down = [(i + 1, i) for i in range(lats - 1)]

    mine = lax.dynamic_slice(
        by_group,
        (t // held * share, 0, t % held, 0, 0, 0),
        (share, lons, 1, group, rows, width),
    )
    mine = jnp.transpose(mine, (1, 2, 3, 0, 4, 5)).reshape(lons * fields, width)
    mixed = vmem_call(
        functools.partial(lat_kernel, lons, share, group, rows, repeat),
        [struct(lons * tall, width)] * (lats // 2),
        [mine, swap(mine, "lat", 1), ahead],
        2 * ahead.shape[0] * 4 * mine.size,
    )
    mixed, later = lax.optimization_barrier(
        (
            mixed,
            (lon_filter, interp_lat, interp_lon, obs_cell, obs_count, obs_value, obs_weight),
        )
    )
    lon_filter, interp_lat, interp_lon, obs_cell, obs_count, obs_value, obs_weight = later
    arrived = [swap(mixed[h], "lat", 2 * h) for h in range(1, lats // 2)]

    rim = cut[-2:]
    before = lax.ppermute(rim[1], "lat", up).reshape(slots, lons, group, 1, share, width)
    after = lax.ppermute(rim[0], "lat", down).reshape(slots, lons, group, 1, share, width)
    rim = jnp.concatenate([before, after], axis=3).reshape(slots, lons, edge, width)
    rims = [rim[0]] + [swap(rim[q], "tm", q) for q in range(1, slots)]

    cap = obs_cell.shape[-1]
    package = vmem_call(
        functools.partial(package_kernel, slots),
        [struct(8, cap)] * slots,
        [obs_count.reshape(slots)] + [x.reshape(slots, cap) for x in (obs_cell, obs_value, obs_weight)],
        0,
        smem=1,
    )
    package = [package[0]] + [swap(package[q], "tm", q) for q in range(1, slots)]
    entries = slots * cap
    fuse = width == entries
    extra = slots * edge
    listing_rows = width + padded + 8
    near = vmem_call(
        functools.partial(list_kernel, lons, slots, width, rows, padded, fuse),
        [struct(listing_rows, entries), struct(extra, width)]
        + [struct(listing_rows + extra if fuse else extra, width)] * (lons - 1),
        [*package, interp_lat, interp_lon, *rims],
        0,
    )
    near, edges = [near[0], *near[2:]], [near[1]]
    for k in range(1, lons):
        sent = near[k]
        near[k] = swap(sent if fuse else near[0], "lon", k)
        edges.append(near[k] if fuse else swap(sent, "lon", k))
    source = []
    for k in range(lons):
        pieces = [lax.dynamic_slice_in_dim(x, (b ^ k) * tall, tall, 0) for x in [mixed[0], *arrived]]
        source.append(functools.reduce(jnp.add, pieces))
    near, _ = lax.optimization_barrier((near, source[1][:1, :1]))
    source = source[:1] + [swap(source[k], "lon", k) for k in range(1, lons)]
    [near] = vmem_call(gather_kernel, [struct(lons, listing_rows, entries)], near, 0)
    listings = [near] + [swap(near, "tm", j) for j in range(1, held)]
    window_rows = held * group * padded
    obs = held * entries
    lists = vmem_call(
        functools.partial(prepare_kernel, lons, held, group, padded, width),
        [
            jax.ShapeDtypeStruct((lons, 2 * width, obs), BF16),
            jax.ShapeDtypeStruct((lons, obs, 2 * width), BF16),
            struct(lons, window_rows, obs),
            struct(lons, 8, obs),
        ],
        listings,
        8 * lons * obs * width,
    )

    tall_table = jnp.concatenate(
        [lax.dynamic_slice_in_dim(lon_filter, (b ^ k) * width, width, 0) for k in range(lons)], axis=0
    )
    table = jnp.concatenate(
        [lax.dynamic_slice_in_dim(tall_table, (b ^ k) * width, width, 1) for k in range(lons)], axis=1
    )
    turned, table, weights, lists = lax.optimization_barrier((table.T, table, weights, lists))
    flops = 4 * tall * whole * whole
    scratch = [pltpu.VMEM((lons, window_rows, width), F32)] * 2
    if parts == 1:
        [spread] = vmem_call(
            functools.partial(middle_kernel, sizes),
            [struct(lons * tall, width)],
            [*source, turned, table, *pert, *edges, *lists],
            2 * flops,
            scratch=scratch,
        )
    else:
        [every] = vmem_call(
            functools.partial(increment_kernel, sizes),
            [struct(lons, slots * group * padded, width)],
            [*source, turned, *pert, *edges],
            flops,
        )
        window = every[:, :window_rows]
        for h in range(1, parts):
            window += swap(every[:, h * window_rows : (h + 1) * window_rows], "tm", h * held)
        [grad] = vmem_call(
            functools.partial(observe_kernel, sizes),
            [struct(lons, window_rows, width)],
            [window, *lists],
            8 * window_rows * whole * obs,
        )
        grads = [grad] + [swap(grad, "tm", h * held) for h in range(1, parts)]
        [spread] = vmem_call(
            functools.partial(adjoint_kernel, sizes, parts),
            [struct(lons * tall, width)],
            [*grads, table, *pert, *edges],
            flops,
        )
    out = vmem_call(
        functools.partial(lat_back_kernel, lons, share, group, rows, repeat),
        [struct(fields, width)] * (lons * (lats // 2)),
        [spread, swap(spread, "lat", 1), weights],
        2 * weights.shape[0] * 4 * spread.size,
    )
    result = by_group
    for k in [*range(2, lons), *range(min(lons, 2))]:
        piece = out[k]
        for h in range(1, lats // 2):
            piece = piece + swap(out[h * lons + k], "lat", 2 * h)
        if k > 0:
            piece = swap(piece, "lon", k)
        for q in range(slots):
            here = piece if q == 0 else swap(piece, "tm", q)
            here = jnp.moveaxis(here.reshape(group, share, rows, width), 1, 0)
            here = here.reshape(share, 1, 1, group, rows, width)
            at = ((t ^ q) // held * share, b ^ k, (t ^ q) % held, 0, 0, 0)
            old = lax.dynamic_slice(by_group, at, here.shape)
            result = lax.dynamic_update_slice(result, old + here, at)
    return result.reshape(control.shape)


def solution(mesh):
    placed = (
        P(None, None, "lat", "lon"),
        P("tm", None, None, "lat", "lon"),
        P(),
        P(),
        P("lat", None),
        P("lon", None),
        P("tm", None, "lat", "lon", None),
        P("tm", None, "lat", "lon"),
        P("tm", None, "lat", "lon", None),
        P("tm", None, "lat", "lon", None),
    )
    return jax.shard_map(
        per_device,
        mesh=mesh,
        in_specs=placed,
        out_specs=P(None, None, "lat", "lon"),
        check_vma=False,
    )
```

```python
import functools
import math

import jax
import jax.numpy as jnp
from jax import lax
from jax.experimental import pallas as pl
from jax.experimental.pallas import tpu as pltpu
from jax.sharding import PartitionSpec as P


HIGHEST = lax.Precision.HIGHEST
F32 = jnp.float32
BF16 = jnp.bfloat16


def swap(x, axis, k):
    return lax.ppermute(x, axis, [(i, i ^ k) for i in range(lax.axis_size(axis))])


def split(x):
    high = x.astype(BF16)
    return high, (x - high.astype(F32)).astype(BF16)


def dot(x, y, dims=((1,), (0,)), precision=None):
    return lax.dot_general(
        x, y, (dims, ((), ())), precision=precision, preferred_element_type=F32
    )


def vmem_call(kernel, out_shape, operands, flops, scratch=(), smem=0):
    specs = [pl.BlockSpec(memory_space=pltpu.SMEM)] * smem
    specs += [pl.BlockSpec(memory_space=pltpu.VMEM)] * (len(operands) - smem)
    nbytes = sum(math.prod(x.shape) * x.dtype.itemsize for x in [*operands, *out_shape])
    return pl.pallas_call(
        kernel,
        out_shape=out_shape,
        in_specs=specs,
        out_specs=[pl.BlockSpec(memory_space=pltpu.VMEM)] * len(out_shape),
        scratch_shapes=list(scratch),
        cost_estimate=pl.CostEstimate(flops=flops, bytes_accessed=nbytes, transcendentals=0),
        compiler_params=pltpu.CompilerParams(vmem_limit_bytes=2 * nbytes + 2**22),
    )(*operands)


def struct(*shape):
    return jax.ShapeDtypeStruct(shape, F32)


def cut_kernel(bands, slots, share, group, *refs):
    pert, outs, first, last = refs[0], refs[1:-2], refs[-2], refs[-1]
    rows, width = pert.shape[4:]
    t, b = lax.axis_index("tm"), lax.axis_index("lon")
    held = pert.shape[2]
    for q in range(slots):
        member = lax.div(t ^ q, held) * share
        level = lax.rem(t ^ q, held)
        for k in range(bands):
            for inner in range(group):
                part = pert[pl.ds(member, share), b ^ k, level, inner]
                part = part.astype(F32)
                at = inner * share * rows
                outs[q * bands + k][at : at + share * rows, :] = part.reshape(share * rows, width)
                at = ((q * bands + k) * group + inner) * share
                first[at : at + share, :] = part[:, 0, :]
                last[at : at + share, :] = part[:, rows - 1, :]


def weight_kernel(lats, rows, repeat, matrix, ahead, back):
    a = lax.axis_index("lat")
    length = matrix.shape[1]
    size = repeat * rows
    full = size + 2 * repeat
    iota = lax.broadcasted_iota

    def pick(shape, axis, wanted):
        return jnp.where(iota(jnp.int32, shape, axis) == wanted, 1.0, 0.0).astype(BF16)

    def block(to, of):
        line = iota(jnp.int32, (full, length), 0)
        rim = line - size
        wanted = jnp.where(
            rim < 0,
            to * rows + jnp.bitwise_and(line, rows - 1),
            to * rows + jnp.where(rim < repeat, -1, rows),
        )
        chosen = dot(pick((full, length), 1, wanted), matrix[...]).astype(BF16)
        column = iota(jnp.int32, (length, size), 1)
        chosen = dot(chosen, pick((length, size), 0, of * rows + jnp.bitwise_and(column, rows - 1)))
        line, column = iota(jnp.int32, (full, size), 0), iota(jnp.int32, (full, size), 1)
        rim = line - size
        field = jnp.where(rim < 0, line // rows, jnp.bitwise_and(rim, repeat - 1))
        return jnp.where(field == column // rows, chosen, 0.0)

    for h in range(0, lats, 2):
        at = h // 2 * full
        wide = jnp.concatenate([block(a ^ h, a ^ j) for j in (0, 1)], axis=1)
        ahead[at : at + full, :] = jnp.concatenate([wide, wide], axis=1).astype(BF16)
        at = h // 2 * size
        wide = jnp.concatenate([block(a ^ j, a ^ h).T for j in (0, 1)], axis=1)
        back[at : at + size, :] = jnp.concatenate([wide, wide], axis=1).astype(BF16)


def package_kernel(slots, count, cell, value, weight, *outs):
    t = lax.axis_index("tm")
    cap = cell.shape[1]
    entry = lax.broadcasted_iota(jnp.int32, (1, cap), 1)
    for q in range(slots):
        slot = t ^ q
        at = pl.ds(slot, 1)
        usable = jnp.where(entry < count[slot], 1.0, 0.0)
        lines = [cell[at, :].astype(F32), value[at, :], weight[at, :] * usable]
        outs[q][...] = jnp.concatenate(lines + [jnp.zeros((5, cap), F32)], axis=0)


def list_kernel(slots, held, half, *refs):
    package, interp, outs, turned = refs[:slots], refs[slots], refs[slots + 1 : -1], refs[-1]
    count, cap = interp.shape[0], package[0].shape[1]
    cols = interp.shape[1] // held
    part = lax.rem(lax.axis_index("tm"), held)
    mine = interp[:, :cols]
    for n in range(1, held):
        mine = jnp.where(part == n, interp[:, n * cols : (n + 1) * cols], mine)
    turned[...] = jnp.concatenate(
        [
            mine[1 : count - 1],
            mine[:1],
            mine[count - 1 :],
            jnp.zeros((turned.shape[0] - count, cols), F32),
        ],
        axis=0,
    )
    start = jnp.bitwise_and(lax.axis_index("lat"), 1) * (turned.shape[0] - half)
    outs[0][:half, :] = turned[pl.ds(pl.multiple_of(start, 8), half), :]
    at = outs[-1].shape[0] - 8
    for h in range(slots):
        outs[-1][at:, h * cap : (h + 1) * cap] = package[h][...]


def merge_kernel(bands, fields, *refs):
    rims, parts, outs = refs[:fields], refs[fields:-bands], refs[-bands:]
    edge = rims[0].shape[1]
    tall = outs[0].shape[0] - len(rims) * edge
    b = lax.axis_index("lon")
    for k in range(bands):
        at = pl.ds(pl.multiple_of((b ^ k) * tall, 8), tall)
        total = parts[0][at, :]
        for part in parts[1:]:
            total = total + part[at, :]
        outs[k][:tall, :] = total
        for q, rim in enumerate(rims):
            outs[k][tall + q * edge : tall + (q + 1) * edge, :] = rim[k]


def gather_kernel(*refs):
    out = refs[-1]
    for k, ref in enumerate(refs[:-1]):
        out[k] = ref[: out.shape[1], :]


def finish_kernel(bands, slots, share, group, control, *refs):
    pieces, out = refs[:-1], refs[-1]
    rows, width = control.shape[4:]
    t, b = lax.axis_index("tm"), lax.axis_index("lon")
    held = control.shape[2]
    for q in range(slots):
        member = pl.ds(lax.div(t ^ q, held) * share, share)
        level = lax.rem(t ^ q, held)
        for k in range(bands):
            for inner in range(group):
                at = inner * share * rows
                part = pieces[q * bands + k][at : at + share * rows, :].reshape(share, rows, width)
                old = control[member, b ^ k, level, inner]
                out[member, b ^ k, level, inner] = old + part


def pairs(blocks):
    return [
        blocks[i] if i + 1 == len(blocks) else jnp.concatenate(blocks[i : i + 2], axis=1)
        for i in range(0, len(blocks), 2)
    ]


def lat_kernel(share, group, rows, repeat, own, other, weights, *outs):
    table = weights[...]
    size, width = repeat * rows, own.shape[1]
    full = size + 2 * repeat
    fields = group * share * rows
    tall = fields + 2 * group * share
    blocks = []
    for i in range(own.shape[0] // size):
        block = jnp.concatenate([ref[i * size : (i + 1) * size, :] for ref in (own, other)], axis=0)
        blocks.append(block)
    for pair, block in enumerate(pairs(blocks)):
        result = dot(table, jnp.concatenate(split(block), axis=0))
        for side in range(block.shape[1] // width):
            line = (2 * pair + side) * repeat
            band, inner, member = line // (group * share), line // share % group, line % share
            at = band * tall + (inner * share + member) * rows
            span = slice(side * width, (side + 1) * width)
            for h, out in enumerate(outs):
                base = h * full
                out[at : at + size, :] = result[base : base + size, span]
                for rim in (0, 1):
                    to = band * tall + fields + (2 * inner + rim) * share + member
                    of = base + size + rim * repeat
                    out[to : to + repeat, :] = result[of : of + repeat, span]


def lat_back_kernel(bands, share, group, rows, repeat, own, other, weights, *outs):
    table = weights[...]
    size, width = repeat * rows, own.shape[1]
    fields = group * share * rows
    tall = fields + 2 * group * share
    blocks, where = [], []
    for k in range(bands):
        for inner in range(group):
            for member in range(0, share, repeat):
                block = []
                for ref in (own, other):
                    at = k * tall + (inner * share + member) * rows
                    block.append(ref[at : at + size, :])
                    for rim in (0, 1):
                        at = k * tall + fields + (2 * inner + rim) * share + member
                        block.append(ref[at : at + repeat, :])
                blocks.append(jnp.concatenate(block, axis=0))
                where.append((k, (inner * share + member) * rows))
    for pair, block in enumerate(pairs(blocks)):
        result = dot(table, jnp.concatenate(split(block), axis=0))
        for side in range(block.shape[1] // width):
            k, at = where[2 * pair + side]
            span = slice(side * width, (side + 1) * width)
            for h in range(len(outs) // bands):
                outs[h * bands + k][at : at + size, :] = result[h * size : (h + 1) * size, span]


def increment_stage(sizes, source, table, pert, rims, window):
    bands, slots, share, group, rows, padded, width = sizes
    fields = group * share * rows
    pieces = [split(f[: fields + 2 * group * share, :]) for f in source]
    high, low = (jnp.concatenate([p[i] for p in pieces], axis=1) for i in (0, 1))
    part = table[...]
    spread = dot(high, part) + dot(low, part)
    filler = jnp.zeros((padded - rows - 2, width), F32)
    for q in range(slots):
        for k in range(bands):
            span = slice(k * width, (k + 1) * width)
            for inner in range(group):
                total = None
                for m in range(share):
                    at = (inner * share + m) * rows
                    term = spread[at : at + rows, span] * pert[q * bands + k][at : at + rows, :]
                    total = term if total is None else total + term
                block = [total]
                for rim in (0, 1):
                    at = (2 * inner + rim) * share
                    at_edge = rims[k].shape[0] + (q - slots) * 2 * group * share + at
                    edge = rims[k][at_edge : at_edge + share, :]
                    edge = spread[fields + at : fields + at + share, span] * edge
                    block.append(jnp.sum(edge, axis=0, keepdims=True))
                at = (q * group + inner) * padded
                window[k, at : at + padded, :] = jnp.concatenate(block + [filler], axis=0)


def observe_stage(sizes, window, tables, grad):
    bands, _, _, _, _, _, width = sizes
    onto, back, chosen, ends = tables
    tall = chosen.shape[1]
    lane = lax.broadcasted_iota(jnp.int32, (tall, width), 1)
    b = lax.axis_index("lon")
    for k in range(bands):
        grad[k] = jnp.zeros((tall, width), F32)
    for k in range(bands):
        before = b ^ lax.rem((b ^ k) + bands - 1, bands)
        after = b ^ lax.rem((b ^ k) + 1, bands)
        upper, lower = split(window[k])
        table = onto[k]
        left, right = ends[k, 0:1], ends[k, 1:2]
        seen_by = dot(jnp.concatenate([upper, upper], axis=1), table) + dot(lower, table[:width])
        seen_by += window[before][:, width - 1 : width] * left
        seen_by += window[after][:, 0:1] * right
        pick = chosen[k]
        seen = jnp.sum(pick * seen_by, axis=0, keepdims=True)
        weighted = pick * (ends[k, 4:5] * (seen - ends[k, 3:4]))
        upper, lower = split(weighted)
        table = back[k]
        both = dot(upper, table)
        grad[k] += both[:, :width] + both[:, width:] + dot(lower, table[:, :width])
        onto_left = jnp.sum(weighted * left, axis=1, keepdims=True)
        onto_right = jnp.sum(weighted * right, axis=1, keepdims=True)
        grad[before] += jnp.where(lane == width - 1, onto_left, 0.0)
        grad[after] += jnp.where(lane == 0, onto_right, 0.0)


def adjoint_stage(sizes, grads, table, pert, rims, outs):
    bands, slots, share, group, rows, padded, width = sizes
    held = slots // len(grads)
    fields = group * share * rows
    columns = []
    for k in range(bands):
        pieces = []
        for inner in range(group):
            lines = [
                grads[q // held][k, pl.ds((q % held * group + inner) * padded, padded), :]
                for q in range(slots)
            ]
            for m in range(share):
                at = (inner * share + m) * rows
                pieces.append(sum(
                    lines[q][:rows] * pert[q * bands + k][at : at + rows, :] for q in range(slots)
                ))
        for inner in range(group):
            for rim in (0, 1):
                at = (2 * inner + rim) * share
                total = 0.0
                for q in range(slots):
                    line = (q % held * group + inner) * padded + rows + rim
                    line = grads[q // held][k, line : line + 1, :]
                    edge = rims[k].shape[0] + (q - slots) * 2 * group * share + at
                    total += line * rims[k][edge : edge + share, :]
                pieces.append(total)
        columns.append(split(jnp.concatenate(pieces, axis=0)))
    high, low = (jnp.concatenate([c[i] for c in columns], axis=1) for i in (0, 1))
    part = table[...]
    result = dot(high, part) + dot(low, part)
    tall = fields + 2 * group * share
    for k in range(bands):
        out, at = (outs[1], 0) if len(outs) > 1 and k == bands - 1 else (outs[0], k * tall)
        out[at : at + tall, :] = result[:, k * width : (k + 1) * width]


def middle_kernel(sizes, *refs):
    bands, slots = sizes[:2]
    source, turned, table, rest = refs[:bands], refs[bands], refs[bands + 1], refs[bands + 2 :]
    pert, rims, rest = rest[: slots * bands], source, rest[slots * bands :]
    tables, outs, (window, grad) = rest[:4], rest[4:-2], rest[-2:]
    increment_stage(sizes, source, turned, pert, rims, window)
    observe_stage(sizes, window, tables, grad)
    adjoint_stage(sizes, [grad], table, pert, rims, outs)


def increment_kernel(sizes, *refs):
    bands = sizes[0]
    pert, out = refs[bands + 1 : -1], refs[-1]
    increment_stage(sizes, refs[:bands], refs[bands], pert, refs[:bands], out)


def observe_kernel(sizes, window, onto, back, chosen, ends, grad):
    observe_stage(sizes, window, (onto, back, chosen, ends), grad)


def adjoint_kernel(sizes, sets, *refs):
    bands, slots = sizes[:2]
    grads, table, rest = refs[:sets], refs[sets], refs[sets + 1 :]
    pert, rest = rest[: bands * slots], rest[bands * slots :]
    adjoint_stage(sizes, grads, table, pert, rest[:bands], rest[bands:])


def prepare_kernel(sizes, held, half, fine, *refs):
    bands, _, _, levels, rows, padded, width = sizes
    parts, packs, interp_lat = refs[: 2 * held], refs[2 * held : 3 * held], refs[3 * held]
    onto, back, chosen, ends, full = refs[3 * held + 1 :]
    fine_rows, fine_cols = fine
    count = packs[0].shape[2]
    obs = held * count
    cols = fine_cols // held
    tm = lax.rem(lax.axis_index("tm"), held)
    first = ((lax.axis_index("lon") * held + tm) * levels).astype(F32)
    parity = jnp.bitwise_and(lax.axis_index("lat"), 1)
    lat = interp_lat[...]
    lat = jnp.concatenate(
        [lat[1 : rows + 1], lat[:1], lat[rows + 1 :], jnp.zeros((padded - rows - 2, fine_rows), F32)], axis=0
    )
    slot = lax.broadcasted_iota(jnp.int32, (1, obs), 1) // count
    for k in range(bands):
        base = packs[0].shape[1] - 8
        lines = jnp.concatenate([pack[k, base:, :] for pack in packs], axis=1)
        cell = lines[0:1] + 0.5
        level = jnp.floor(cell * (1.0 / (fine_rows * fine_cols)))
        inside = cell - level * (fine_rows * fine_cols)
        row = jnp.floor(inside * (1.0 / fine_cols))
        col = jnp.floor(inside - row * fine_cols).astype(jnp.int32)
        line = lax.broadcasted_iota(jnp.int32, (cols, obs), 0)
        hot = [
            jnp.where(line == col - jnp.bitwise_xor(tm, j) * cols, 1.0, 0.0).astype(BF16)
            for j in range(held)
        ]
        hot = jnp.concatenate(hot, axis=0)
        for side in (0, 1):
            part = jnp.concatenate([parts[2 * j + side][k, :half, :] for j in range(held)], axis=1)
            upper, lower = split(part)
            start = jnp.bitwise_xor(parity, side) * (full.shape[0] - half)
            full[pl.ds(pl.multiple_of(start, 8), half), :] = dot(upper, hot) + dot(lower, hot)
        main = full[:width, :]
        upper, lower = split(main)
        onto[k, :width, :] = upper
        onto[k, width:, :] = lower
        upper, lower = split(main.T)
        back[k, :, :width] = upper
        back[k, :, width:] = lower
        line = lax.broadcasted_iota(jnp.int32, (fine_rows, obs), 0)
        hot = jnp.where(line == row.astype(jnp.int32), 1.0, 0.0)
        rowpart = dot(lat, hot, precision=HIGHEST)
        ends[k] = jnp.concatenate([full[width : width + 2, :], level, lines[1:3], lines[3:6]], axis=0)
        for j in range(held):
            for inner in range(levels):
                at = (j * levels + inner) * padded
                fits = jnp.logical_and(level == first + inner, slot == j)
                chosen[k, at : at + padded, :] = jnp.where(fits, rowpart, 0.0)


def per_device(
    control,
    ens_pert,
    lat_filter,
    lon_filter,
    interp_lat,
    interp_lon,
    obs_cell,
    obs_count,
    obs_value,
    obs_weight,
):
    slots, lats, lons = (lax.axis_size(axis) for axis in ("tm", "lat", "lon"))
    t, _, b = (lax.axis_index(axis) for axis in ("tm", "lat", "lon"))
    members, levels, rows, width = control.shape
    held = math.gcd(slots, levels // lons)
    parts = slots // held
    share = members // parts
    group = levels // (lons * held)
    fields = group * share * rows
    edge = 2 * group * share
    tall = fields + edge
    whole = lons * width
    padded = -(-(rows + 2) // 8) * 8
    sizes = (lons, slots, share, group, rows, padded, width)
    split_up = (members, lons, held, group, rows, width)
    by_group = control.reshape(split_up)

    repeat = math.gcd(share, max(64 // rows, 1))

    size = repeat * rows
    full = size + 2 * repeat
    ahead, weights = vmem_call(
        functools.partial(weight_kernel, lats, rows, repeat),
        [
            jax.ShapeDtypeStruct((lats // 2 * full, 4 * size), BF16),
            jax.ShapeDtypeStruct((lats // 2 * size, 4 * full), BF16),
        ],
        [lat_filter],
        0,
    )

    count = slots * lons
    cut = vmem_call(
        functools.partial(cut_kernel, lons, slots, share, group),
        [struct(fields, width)] * count + [struct(count * group * share, width)] * 2,
        [ens_pert[0].reshape(split_up)],
        0,
    )
    pert = [None] * count
    order = [*range(2, lons), *range(1, min(lons, 2)), 0]
    for k in order:
        for q in range(slots):
            piece = cut[q * lons + k]
            if q > 0:
                piece = swap(piece, "tm", q)
            pert[q * lons + k] = piece if k == 0 else swap(piece, "lon", k)
    up = [(i, i + 1) for i in range(lats - 1)]
    down = [(i + 1, i) for i in range(lats - 1)]

    mine = lax.dynamic_slice(
        by_group,
        (t // held * share, 0, t % held, 0, 0, 0),
        (share, lons, 1, group, rows, width),
    )
    mine = jnp.transpose(mine, (1, 2, 3, 0, 4, 5)).reshape(lons * fields, width)
    mixed = vmem_call(
        functools.partial(lat_kernel, share, group, rows, repeat),
        [struct(lons * tall, width)] * (lats // 2),
        [mine, swap(mine, "lat", 1), ahead],
        2 * ahead.shape[0] * 4 * mine.size,
    )
    arrived = [swap(mixed[h], "lat", 2 * h) for h in range(1, lats // 2)]

    rim = cut[-2:]
    before = lax.ppermute(rim[1], "lat", up).reshape(slots, lons, group, 1, share, width)
    after = lax.ppermute(rim[0], "lat", down).reshape(slots, lons, group, 1, share, width)
    rim = jnp.concatenate([before, after], axis=3).reshape(slots, lons, edge, width)
    rims = [rim[0]] + [swap(rim[q], "tm", q) for q in range(1, slots)]

    cap = obs_cell.shape[-1]
    package = vmem_call(
        functools.partial(package_kernel, slots),
        [struct(8, cap)] * slots,
        [obs_count.reshape(slots)] + [x.reshape(slots, cap) for x in (obs_cell, obs_value, obs_weight)],
        0,
        smem=1,
    )
    package = [package[0]] + [swap(package[q], "tm", q) for q in range(1, slots)]
    entries = slots * cap
    fine = interp_lat.shape[0], interp_lon.shape[0]
    cols = fine[1] // held
    turned_rows = -(-(width + 2) // 8) * 8
    half = -(-turned_rows // 16) * 8
    fuse = entries == cols
    shapes = [struct(half + 8, cols)] if fuse else [struct(half, cols), struct(8, entries)]
    listing = vmem_call(
        functools.partial(list_kernel, slots, held, half),
        shapes,
        [*package, interp_lon.T],
        0,
        scratch=[pltpu.VMEM((turned_rows, cols), F32)],
    )
    near = [[x] + [swap(x, "lon", k) for k in range(1, lons)] for x in listing]
    source = vmem_call(
        functools.partial(merge_kernel, lons, slots),
        [struct(tall + slots * edge, width)] * lons,
        [*rims, mixed[0], *arrived],
        0,
    )
    source = [source[0]] + [swap(source[k], "lon", k) for k in range(1, lons)]
    near = [vmem_call(gather_kernel, [struct(lons, *x[0].shape)], x, 0)[0] for x in near]
    slices, packs = [], []
    for j in range(held):
        here = near if j == 0 else [swap(x, "tm", j) for x in near]
        slices += [here[0], swap(here[0], "lat", 1)]
        packs.append(here[-1])
    window_rows = held * group * padded
    obs = held * entries
    lists = vmem_call(
        functools.partial(prepare_kernel, sizes, held, half, fine),
        [
            jax.ShapeDtypeStruct((lons, 2 * width, obs), BF16),
            jax.ShapeDtypeStruct((lons, obs, 2 * width), BF16),
            struct(lons, window_rows, obs),
            struct(lons, 8, obs),
        ],
        [*slices, *packs, interp_lat.T],
        8 * lons * obs * width * fine[1],
        scratch=[pltpu.VMEM((turned_rows, obs), F32)],
    )

    tall_table = jnp.concatenate(
        [lax.dynamic_slice_in_dim(lon_filter, (b ^ k) * width, width, 0) for k in range(lons)], axis=0
    )
    table = jnp.concatenate(
        [lax.dynamic_slice_in_dim(tall_table, (b ^ k) * width, width, 1) for k in range(lons)], axis=1
    )
    turned = table.T
    flops = 4 * tall * whole * whole
    scratch = [pltpu.VMEM((lons, window_rows, width), F32)] * 2
    early = max(lons - 1, 1)
    shapes = [struct(early * tall, width)] + [struct(tall, width)] * (lons - early)
    if parts == 1:
        spread = vmem_call(
            functools.partial(middle_kernel, sizes),
            shapes,
            [*source, turned, table, *pert, *lists],
            2 * flops,
            scratch=scratch,
        )
    else:
        [every] = vmem_call(
            functools.partial(increment_kernel, sizes),
            [struct(lons, slots * group * padded, width)],
            [*source, turned, *pert],
            flops,
        )
        window = every[:, :window_rows]
        for h in range(1, parts):
            window += swap(every[:, h * window_rows :][:, :window_rows], "tm", h * held)
        [grad] = vmem_call(
            functools.partial(observe_kernel, sizes),
            [struct(lons, window_rows, width)],
            [window, *lists],
            8 * window_rows * whole * obs,
        )
        grads = [grad] + [swap(grad, "tm", h * held) for h in range(1, parts)]
        spread = vmem_call(
            functools.partial(adjoint_kernel, sizes, parts), shapes, [*grads, table, *pert, *source], flops
        )

    def lat_back(x, count):
        out = vmem_call(
            functools.partial(lat_back_kernel, count, share, group, rows, repeat),
            [struct(fields, width)] * (count * (lats // 2)),
            [x, swap(x, "lat", 1), weights],
            8 * weights.shape[0] * x.size,
        )
        pieces = []
        for n in range(count):
            piece = out[n]
            for h in range(1, lats // 2):
                piece = piece + swap(out[h * count + n], "lat", 2 * h)
            pieces.append(piece)
        return pieces

    done = {}
    for k, piece in enumerate(lat_back(spread[0], early)):
        done[k] = swap(piece, "lon", k) if k > 0 else piece
    if early < lons:
        piece = swap(spread[1], "lon", early)
        [done[early]] = lat_back(piece, 1)
    arrived = {}
    for k in done:
        arrived[k, 0] = done[k]
        for q in range(1, slots):
            arrived[k, q] = swap(done[k], "tm", q)
    pieces = [arrived[k, q] for q in range(slots) for k in range(lons)]
    [result] = vmem_call(
        functools.partial(finish_kernel, lons, slots, share, group),
        [struct(*split_up)],
        [by_group, *pieces],
        control.size,
    )
    return result.reshape(control.shape)


def solution(mesh):
    placed = (
        P(None, None, "lat", "lon"),
        P("tm", None, None, "lat", "lon"),
        P(),
        P(),
        P("lat", None),
        P("lon", None),
        P("tm", None, "lat", "lon", None),
        P("tm", None, "lat", "lon"),
        P("tm", None, "lat", "lon", None),
        P("tm", None, "lat", "lon", None),
    )
    return jax.shard_map(
        per_device,
        mesh=mesh,
        in_specs=placed,
        out_specs=P(None, None, "lat", "lon"),
        check_vma=False,
    )
```

```python
import functools
import math

import jax
import jax.numpy as jnp
from jax import lax
from jax.experimental import pallas as pl
from jax.experimental.pallas import tpu as pltpu
from jax.sharding import PartitionSpec as P


HIGHEST = lax.Precision.HIGHEST
F32 = jnp.float32
BF16 = jnp.bfloat16


def swap(x, axis, k):
    return lax.ppermute(x, axis, [(i, i ^ k) for i in range(lax.axis_size(axis))])


def split(x):
    high = x.astype(BF16)
    return high, (x - high.astype(F32)).astype(BF16)


def dot(x, y, dims=((1,), (0,)), precision=None):
    return lax.dot_general(
        x, y, (dims, ((), ())), precision=precision, preferred_element_type=F32
    )


def vmem_call(kernel, out_shape, operands, flops, scratch=(), smem=0):
    specs = [pl.BlockSpec(memory_space=pltpu.SMEM)] * smem
    specs += [pl.BlockSpec(memory_space=pltpu.VMEM)] * (len(operands) - smem)
    nbytes = sum(math.prod(x.shape) * x.dtype.itemsize for x in [*operands, *out_shape])
    return pl.pallas_call(
        kernel,
        out_shape=out_shape,
        in_specs=specs,
        out_specs=[pl.BlockSpec(memory_space=pltpu.VMEM)] * len(out_shape),
        scratch_shapes=list(scratch),
        cost_estimate=pl.CostEstimate(flops=flops, bytes_accessed=nbytes, transcendentals=0),
        compiler_params=pltpu.CompilerParams(vmem_limit_bytes=2 * nbytes + 2**22),
    )(*operands)


def struct(*shape):
    return jax.ShapeDtypeStruct(shape, F32)


def cut_kernel(bands, slots, share, group, *refs):
    pert, outs, first, last = refs[0], refs[1:-2], refs[-2], refs[-1]
    rows, width = pert.shape[4:]
    t, b = lax.axis_index("tm"), lax.axis_index("lon")
    held = pert.shape[2]
    for q in range(slots):
        member = lax.div(t ^ q, held) * share
        level = lax.rem(t ^ q, held)
        for k in range(bands):
            for inner in range(group):
                part = pert[pl.ds(member, share), b ^ k, level, inner]
                part = part.astype(F32)
                at = inner * share * rows
                outs[q * bands + k][at : at + share * rows, :] = part.reshape(share * rows, width)
                at = ((q * bands + k) * group + inner) * share
                first[at : at + share, :] = part[:, 0, :]
                last[at : at + share, :] = part[:, rows - 1, :]


def weight_kernel(lats, rows, repeat, matrix, ahead, back):
    a = lax.axis_index("lat")
    length = matrix.shape[1]
    size = repeat * rows
    full = size + 2 * repeat
    iota = lax.broadcasted_iota

    def pick(shape, axis, wanted):
        return jnp.where(iota(jnp.int32, shape, axis) == wanted, 1.0, 0.0).astype(BF16)

    def block(to, of):
        line = iota(jnp.int32, (full, length), 0)
        rim = line - size
        wanted = jnp.where(
            rim < 0,
            to * rows + jnp.bitwise_and(line, rows - 1),
            to * rows + jnp.where(rim < repeat, -1, rows),
        )
        chosen = dot(pick((full, length), 1, wanted), matrix[...]).astype(BF16)
        column = iota(jnp.int32, (length, size), 1)
        chosen = dot(chosen, pick((length, size), 0, of * rows + jnp.bitwise_and(column, rows - 1)))
        line, column = iota(jnp.int32, (full, size), 0), iota(jnp.int32, (full, size), 1)
        rim = line - size
        field = jnp.where(rim < 0, line // rows, jnp.bitwise_and(rim, repeat - 1))
        return jnp.where(field == column // rows, chosen, 0.0)

    for h in range(0, lats, 2):
        at = h // 2 * full
        wide = jnp.concatenate([block(a ^ h, a ^ j) for j in (0, 1)], axis=1)
        ahead[at : at + full, :] = jnp.concatenate([wide, wide], axis=1).astype(BF16)
        at = h // 2 * size
        wide = jnp.concatenate([block(a ^ j, a ^ h).T for j in (0, 1)], axis=1)
        back[at : at + size, :] = jnp.concatenate([wide, wide], axis=1).astype(BF16)


def package_kernel(slots, count, cell, value, weight, *outs):
    t = lax.axis_index("tm")
    cap = cell.shape[1]
    entry = lax.broadcasted_iota(jnp.int32, (1, cap), 1)
    for q in range(slots):
        slot = t ^ q
        at = pl.ds(slot, 1)
        usable = jnp.where(entry < count[slot], 1.0, 0.0)
        lines = [cell[at, :].astype(F32), value[at, :], weight[at, :] * usable]
        outs[q][...] = jnp.concatenate(lines + [jnp.zeros((5, cap), F32)], axis=0)


def list_kernel(slots, held, half, *refs):
    package, interp, outs, turned = refs[:slots], refs[slots], refs[slots + 1 : -1], refs[-1]
    count, cap = interp.shape[0], package[0].shape[1]
    cols = interp.shape[1] // held
    part = lax.rem(lax.axis_index("tm"), held)
    mine = interp[:, :cols]
    for n in range(1, held):
        mine = jnp.where(part == n, interp[:, n * cols : (n + 1) * cols], mine)
    turned[...] = jnp.concatenate(
        [
            mine[1 : count - 1],
            mine[:1],
            mine[count - 1 :],
            jnp.zeros((turned.shape[0] - count, cols), F32),
        ],
        axis=0,
    )
    start = jnp.bitwise_and(lax.axis_index("lat"), 1) * (turned.shape[0] - half)
    outs[0][:half, :] = turned[pl.ds(pl.multiple_of(start, 8), half), :]
    at = outs[-1].shape[0] - 8
    for h in range(slots):
        outs[-1][at:, h * cap : (h + 1) * cap] = package[h][...]


def merge_kernel(bands, fields, *refs):
    rims, parts, outs = refs[:fields], refs[fields:-bands], refs[-bands:]
    edge = rims[0].shape[1]
    tall = outs[0].shape[0] - len(rims) * edge
    b = lax.axis_index("lon")
    for k in range(bands):
        at = pl.ds(pl.multiple_of((b ^ k) * tall, 8), tall)
        total = parts[0][at, :]
        for part in parts[1:]:
            total = total + part[at, :]
        outs[k][:tall, :] = total
        for q, rim in enumerate(rims):
            outs[k][tall + q * edge : tall + (q + 1) * edge, :] = rim[k]


def gather_kernel(*refs):
    out = refs[-1]
    for k, ref in enumerate(refs[:-1]):
        out[k] = ref[: out.shape[1], :]


def finish_kernel(bands, slots, share, group, control, *refs):
    pieces, out = refs[:-1], refs[-1]
    rows, width = control.shape[4:]
    t, b = lax.axis_index("tm"), lax.axis_index("lon")
    held = control.shape[2]
    for q in range(slots):
        member = pl.ds(lax.div(t ^ q, held) * share, share)
        level = lax.rem(t ^ q, held)
        for k in range(bands):
            for inner in range(group):
                at = inner * share * rows
                part = pieces[q * bands + k][at : at + share * rows, :].reshape(share, rows, width)
                old = control[member, b ^ k, level, inner]
                out[member, b ^ k, level, inner] = old + part


def spin_kernel(bands, matrix, table, turned):
    b = lax.axis_index("lon")
    width = matrix.shape[0] // bands
    for k in range(bands):
        at = pl.ds(pl.multiple_of((b ^ k) * width, width), width)
        for j in range(bands):
            block = matrix[at, pl.ds(pl.multiple_of((b ^ j) * width, width), width)]
            ks, js = slice(k * width, (k + 1) * width), slice(j * width, (j + 1) * width)
            table[ks, js] = block
            turned[js, ks] = block.astype(F32).T.astype(BF16)


def pairs(blocks):
    return [
        blocks[i] if i + 1 == len(blocks) else jnp.concatenate(blocks[i : i + 2], axis=1)
        for i in range(0, len(blocks), 2)
    ]


def lat_kernel(share, group, rows, repeat, own, other, weights, *outs):
    table = weights[...]
    size, width = repeat * rows, own.shape[1]
    full = size + 2 * repeat
    fields = group * share * rows
    tall = fields + 2 * group * share
    blocks = []
    for i in range(own.shape[0] // size):
        block = jnp.concatenate([ref[i * size : (i + 1) * size, :] for ref in (own, other)], axis=0)
        blocks.append(block)
    for pair, block in enumerate(pairs(blocks)):
        result = dot(table, jnp.concatenate(split(block), axis=0))
        for side in range(block.shape[1] // width):
            line = (2 * pair + side) * repeat
            band, inner, member = line // (group * share), line // share % group, line % share
            at = band * tall + (inner * share + member) * rows
            span = slice(side * width, (side + 1) * width)
            for h, out in enumerate(outs):
                base = h * full
                out[at : at + size, :] = result[base : base + size, span]
                for rim in (0, 1):
                    to = band * tall + fields + (2 * inner + rim) * share + member
                    of = base + size + rim * repeat
                    out[to : to + repeat, :] = result[of : of + repeat, span]


def lat_back_kernel(bands, share, group, rows, repeat, own, other, weights, *outs):
    table = weights[...]
    size, width = repeat * rows, own.shape[1]
    fields = group * share * rows
    tall = fields + 2 * group * share
    blocks, where = [], []
    for k in range(bands):
        for inner in range(group):
            for member in range(0, share, repeat):
                block = []
                for ref in (own, other):
                    at = k * tall + (inner * share + member) * rows
                    block.append(ref[at : at + size, :])
                    for rim in (0, 1):
                        at = k * tall + fields + (2 * inner + rim) * share + member
                        block.append(ref[at : at + repeat, :])
                blocks.append(jnp.concatenate(block, axis=0))
                where.append((k, (inner * share + member) * rows))
    for pair, block in enumerate(pairs(blocks)):
        result = dot(table, jnp.concatenate(split(block), axis=0))
        for side in range(block.shape[1] // width):
            k, at = where[2 * pair + side]
            span = slice(side * width, (side + 1) * width)
            for h in range(len(outs) // bands):
                outs[h * bands + k][at : at + size, :] = result[h * size : (h + 1) * size, span]


def increment_stage(sizes, source, table, pert, rims, window):
    bands, slots, share, group, rows, padded, width = sizes
    fields = group * share * rows
    pieces = [split(f[: fields + 2 * group * share, :]) for f in source]
    high, low = (jnp.concatenate([p[i] for p in pieces], axis=1) for i in (0, 1))
    part = table[...]
    spread = dot(high, part) + dot(low, part)
    filler = jnp.zeros((padded - rows - 2, width), F32)
    for q in range(slots):
        for k in range(bands):
            span = slice(k * width, (k + 1) * width)
            for inner in range(group):
                total = None
                for m in range(share):
                    at = (inner * share + m) * rows
                    term = spread[at : at + rows, span] * pert[q * bands + k][at : at + rows, :]
                    total = term if total is None else total + term
                block = [total]
                for rim in (0, 1):
                    at = (2 * inner + rim) * share
                    at_edge = rims[k].shape[0] + (q - slots) * 2 * group * share + at
                    edge = rims[k][at_edge : at_edge + share, :]
                    edge = spread[fields + at : fields + at + share, span] * edge
                    block.append(jnp.sum(edge, axis=0, keepdims=True))
                at = (q * group + inner) * padded
                window[k, at : at + padded, :] = jnp.concatenate(block + [filler], axis=0)


def observe_stage(sizes, window, tables, grad):
    bands, _, _, _, _, _, width = sizes
    onto, back, chosen, ends = tables
    tall = chosen.shape[1]
    lane = lax.broadcasted_iota(jnp.int32, (tall, width), 1)
    b = lax.axis_index("lon")
    for k in range(bands):
        grad[k] = jnp.zeros((tall, width), F32)
    for k in range(bands):
        before = b ^ lax.rem((b ^ k) + bands - 1, bands)
        after = b ^ lax.rem((b ^ k) + 1, bands)
        upper, lower = split(window[k])
        table = onto[k]
        left, right = ends[k, 0:1], ends[k, 1:2]
        seen_by = dot(jnp.concatenate([upper, upper], axis=1), table) + dot(lower, table[:width])
        seen_by += window[before][:, width - 1 : width] * left
        seen_by += window[after][:, 0:1] * right
        pick = chosen[k]
        seen = jnp.sum(pick * seen_by, axis=0, keepdims=True)
        weighted = pick * (ends[k, 4:5] * (seen - ends[k, 3:4]))
        upper, lower = split(weighted)
        table = back[k]
        both = dot(upper, table)
        grad[k] += both[:, :width] + both[:, width:] + dot(lower, table[:, :width])
        onto_left = jnp.sum(weighted * left, axis=1, keepdims=True)
        onto_right = jnp.sum(weighted * right, axis=1, keepdims=True)
        grad[before] += jnp.where(lane == width - 1, onto_left, 0.0)
        grad[after] += jnp.where(lane == 0, onto_right, 0.0)


def adjoint_stage(sizes, grads, table, pert, rims, outs):
    bands, slots, share, group, rows, padded, width = sizes
    held = slots // len(grads)
    fields = group * share * rows
    columns = []
    for k in range(bands):
        pieces = []
        for inner in range(group):
            lines = [
                grads[q // held][k, pl.ds((q % held * group + inner) * padded, padded), :]
                for q in range(slots)
            ]
            for m in range(share):
                at = (inner * share + m) * rows
                pieces.append(sum(
                    lines[q][:rows] * pert[q * bands + k][at : at + rows, :] for q in range(slots)
                ))
        for inner in range(group):
            for rim in (0, 1):
                at = (2 * inner + rim) * share
                total = 0.0
                for q in range(slots):
                    line = (q % held * group + inner) * padded + rows + rim
                    line = grads[q // held][k, line : line + 1, :]
                    edge = rims[k].shape[0] + (q - slots) * 2 * group * share + at
                    total += line * rims[k][edge : edge + share, :]
                pieces.append(total)
        columns.append(split(jnp.concatenate(pieces, axis=0)))
    high, low = (jnp.concatenate([c[i] for c in columns], axis=1) for i in (0, 1))
    part = table[...]
    result = dot(high, part) + dot(low, part)
    tall = fields + 2 * group * share
    for k in range(bands):
        out, at = (outs[1], 0) if len(outs) > 1 and k == bands - 1 else (outs[0], k * tall)
        out[at : at + tall, :] = result[:, k * width : (k + 1) * width]


def middle_kernel(sizes, *refs):
    bands, slots = sizes[:2]
    source, turned, table, rest = refs[:bands], refs[bands], refs[bands + 1], refs[bands + 2 :]
    pert, rims, rest = rest[: slots * bands], source, rest[slots * bands :]
    tables, outs, (window, grad) = rest[:4], rest[4:-2], rest[-2:]
    increment_stage(sizes, source, turned, pert, rims, window)
    observe_stage(sizes, window, tables, grad)
    adjoint_stage(sizes, [grad], table, pert, rims, outs)


def increment_kernel(sizes, *refs):
    bands = sizes[0]
    pert, out = refs[bands + 1 : -1], refs[-1]
    increment_stage(sizes, refs[:bands], refs[bands], pert, refs[:bands], out)


def observe_kernel(sizes, window, onto, back, chosen, ends, grad):
    observe_stage(sizes, window, (onto, back, chosen, ends), grad)


def adjoint_kernel(sizes, sets, *refs):
    bands, slots = sizes[:2]
    grads, table, rest = refs[:sets], refs[sets], refs[sets + 1 :]
    pert, rest = rest[: bands * slots], rest[bands * slots :]
    adjoint_stage(sizes, grads, table, pert, rest[:bands], rest[bands:])


def prepare_kernel(sizes, held, half, fine, *refs):
    bands, _, _, levels, rows, padded, width = sizes
    parts, packs, interp_lat = refs[: 2 * held], refs[2 * held : 3 * held], refs[3 * held]
    onto, back, chosen, ends, full = refs[3 * held + 1 :]
    fine_rows, fine_cols = fine
    count = packs[0].shape[2]
    obs = held * count
    cols = fine_cols // held
    tm = lax.rem(lax.axis_index("tm"), held)
    first = ((lax.axis_index("lon") * held + tm) * levels).astype(F32)
    parity = jnp.bitwise_and(lax.axis_index("lat"), 1)
    lat = interp_lat[...]
    lat = jnp.concatenate(
        [lat[1 : rows + 1], lat[:1], lat[rows + 1 :], jnp.zeros((padded - rows - 2, fine_rows), F32)], axis=0
    )
    slot = lax.broadcasted_iota(jnp.int32, (1, obs), 1) // count
    for k in range(bands):
        base = packs[0].shape[1] - 8
        lines = jnp.concatenate([pack[k, base:, :] for pack in packs], axis=1)
        cell = lines[0:1] + 0.5
        level = jnp.floor(cell * (1.0 / (fine_rows * fine_cols)))
        inside = cell - level * (fine_rows * fine_cols)
        row = jnp.floor(inside * (1.0 / fine_cols))
        col = jnp.floor(inside - row * fine_cols).astype(jnp.int32)
        line = lax.broadcasted_iota(jnp.int32, (cols, obs), 0)
        hot = [
            jnp.where(line == col - jnp.bitwise_xor(tm, j) * cols, 1.0, 0.0).astype(BF16)
            for j in range(held)
        ]
        hot = jnp.concatenate(hot, axis=0)
        for side in (0, 1):
            part = jnp.concatenate([parts[2 * j + side][k, :half, :] for j in range(held)], axis=1)
            upper, lower = split(part)
            start = jnp.bitwise_xor(parity, side) * (full.shape[0] - half)
            full[pl.ds(pl.multiple_of(start, 8), half), :] = dot(upper, hot) + dot(lower, hot)
        main = full[:width, :]
        upper, lower = split(main)
        onto[k, :width, :] = upper
        onto[k, width:, :] = lower
        upper, lower = split(main.T)
        back[k, :, :width] = upper
        back[k, :, width:] = lower
        line = lax.broadcasted_iota(jnp.int32, (fine_rows, obs), 0)
        hot = jnp.where(line == row.astype(jnp.int32), 1.0, 0.0)
        rowpart = dot(lat, hot, precision=HIGHEST)
        ends[k] = jnp.concatenate([full[width : width + 2, :], level, lines[1:3], lines[3:6]], axis=0)
        for j in range(held):
            for inner in range(levels):
                at = (j * levels + inner) * padded
                fits = jnp.logical_and(level == first + inner, slot == j)
                chosen[k, at : at + padded, :] = jnp.where(fits, rowpart, 0.0)


def per_device(
    control,
    ens_pert,
    lat_filter,
    lon_filter,
    interp_lat,
    interp_lon,
    obs_cell,
    obs_count,
    obs_value,
    obs_weight,
):
    slots, lats, lons = (lax.axis_size(axis) for axis in ("tm", "lat", "lon"))
    t, a, _ = (lax.axis_index(axis) for axis in ("tm", "lat", "lon"))
    members, levels, rows, width = control.shape
    held = math.gcd(slots, levels // lons)
    parts = slots // held
    share = members // parts
    group = levels // (lons * held)
    fields = group * share * rows
    edge = 2 * group * share
    tall = fields + edge
    whole = lons * width
    padded = -(-(rows + 2) // 8) * 8
    sizes = (lons, slots, share, group, rows, padded, width)
    split_up = (members, lons, held, group, rows, width)
    by_group = control.reshape(split_up)

    repeat = math.gcd(share, max(64 // rows, 1))

    size = repeat * rows
    full = size + 2 * repeat
    ahead, weights = vmem_call(
        functools.partial(weight_kernel, lats, rows, repeat),
        [
            jax.ShapeDtypeStruct((lats // 2 * full, 4 * size), BF16),
            jax.ShapeDtypeStruct((lats // 2 * size, 4 * full), BF16),
        ],
        [lat_filter],
        0,
    )

    count = slots * lons
    cut = vmem_call(
        functools.partial(cut_kernel, lons, slots, share, group),
        [struct(fields, width)] * count + [struct(count * group * share, width)] * 2,
        [ens_pert[0].reshape(split_up)],
        0,
    )
    pert = [None] * count
    order = [*range(2, lons), *range(1, min(lons, 2)), 0]
    for k in order:
        for q in range(slots):
            piece = cut[q * lons + k]
            if q > 0:
                piece = swap(piece, "tm", q)
            pert[q * lons + k] = piece if k == 0 else swap(piece, "lon", k)
    mine = lax.dynamic_slice(
        by_group,
        (t // held * share, 0, t % held, 0, 0, 0),
        (share, lons, 1, group, rows, width),
    )
    mine = jnp.transpose(mine, (1, 2, 3, 0, 4, 5)).reshape(lons * fields, width)
    mixed = vmem_call(
        functools.partial(lat_kernel, share, group, rows, repeat),
        [struct(lons * tall, width)] * (lats // 2),
        [mine, swap(mine, "lat", 1), ahead],
        2 * ahead.shape[0] * 4 * mine.size,
    )
    arrived = [swap(mixed[h], "lat", 2 * h) for h in range(1, lats // 2)]

    rim = cut[-2:]
    odd = jnp.bitwise_and(a, 1) == 1
    inside = swap(jnp.where(odd, rim[0], rim[1]), "lat", 1)
    across = [(i, i + 1) for i in range(1, lats - 1, 2)]
    across += [(j, i) for i, j in across]
    outside = lax.ppermute(jnp.where(odd, rim[1], rim[0]), "lat", across)
    form = (slots, lons, group, 1, share, width)
    before = jnp.where(odd, inside, outside).reshape(form)
    after = jnp.where(odd, outside, inside).reshape(form)
    rim = jnp.concatenate([before, after], axis=3).reshape(slots, lons, edge, width)
    rims = [rim[0]] + [swap(rim[q], "tm", q) for q in range(1, slots)]

    cap = obs_cell.shape[-1]
    package = vmem_call(
        functools.partial(package_kernel, slots),
        [struct(8, cap)] * slots,
        [obs_count.reshape(slots)] + [x.reshape(slots, cap) for x in (obs_cell, obs_value, obs_weight)],
        0,
        smem=1,
    )
    package = [package[0]] + [swap(package[q], "tm", q) for q in range(1, slots)]
    entries = slots * cap
    fine = interp_lat.shape[0], interp_lon.shape[0]
    cols = fine[1] // held
    turned_rows = -(-(width + 2) // 8) * 8
    half = -(-turned_rows // 16) * 8
    fuse = entries == cols
    shapes = [struct(half + 8, cols)] if fuse else [struct(half, cols), struct(8, entries)]
    listing = vmem_call(
        functools.partial(list_kernel, slots, held, half),
        shapes,
        [*package, interp_lon.T],
        0,
        scratch=[pltpu.VMEM((turned_rows, cols), F32)],
    )
    near = [[x] + [swap(x, "lon", k) for k in range(1, lons)] for x in listing]
    source = vmem_call(
        functools.partial(merge_kernel, lons, slots),
        [struct(tall + slots * edge, width)] * lons,
        [*rims, mixed[0], *arrived],
        0,
    )
    source = [source[0]] + [swap(source[k], "lon", k) for k in range(1, lons)]
    near = [vmem_call(gather_kernel, [struct(lons, *x[0].shape)], x, 0)[0] for x in near]
    slices, packs = [], []
    for j in range(held):
        here = near if j == 0 else [swap(x, "tm", j) for x in near]
        slices += [here[0], swap(here[0], "lat", 1)]
        packs.append(here[-1])
    window_rows = held * group * padded
    obs = held * entries
    lists = vmem_call(
        functools.partial(prepare_kernel, sizes, held, half, fine),
        [
            jax.ShapeDtypeStruct((lons, 2 * width, obs), BF16),
            jax.ShapeDtypeStruct((lons, obs, 2 * width), BF16),
            struct(lons, window_rows, obs),
            struct(lons, 8, obs),
        ],
        [*slices, *packs, interp_lat.T],
        8 * lons * obs * width * fine[1],
        scratch=[pltpu.VMEM((turned_rows, obs), F32)],
    )

    table, turned = vmem_call(
        functools.partial(spin_kernel, lons),
        [jax.ShapeDtypeStruct((whole, whole), BF16)] * 2,
        [lon_filter],
        0,
    )
    flops = 4 * tall * whole * whole
    scratch = [pltpu.VMEM((lons, window_rows, width), F32)] * 2
    early = max(lons - 1, 1)
    shapes = [struct(early * tall, width)] + [struct(tall, width)] * (lons - early)
    if parts == 1:
        spread = vmem_call(
            functools.partial(middle_kernel, sizes),
            shapes,
            [*source, turned, table, *pert, *lists],
            2 * flops,
            scratch=scratch,
        )
    else:
        [every] = vmem_call(
            functools.partial(increment_kernel, sizes),
            [struct(lons, slots * group * padded, width)],
            [*source, turned, *pert],
            flops,
        )
        window = every[:, :window_rows]
        for h in range(1, parts):
            window += swap(every[:, h * window_rows :][:, :window_rows], "tm", h * held)
        [grad] = vmem_call(
            functools.partial(observe_kernel, sizes),
            [struct(lons, window_rows, width)],
            [window, *lists],
            8 * window_rows * whole * obs,
        )
        grads = [grad] + [swap(grad, "tm", h * held) for h in range(1, parts)]
        spread = vmem_call(
            functools.partial(adjoint_kernel, sizes, parts),
            shapes,
            [*grads, table, *pert, *source],
            flops,
        )

    def lat_back(x, count):
        out = vmem_call(
            functools.partial(lat_back_kernel, count, share, group, rows, repeat),
            [struct(fields, width)] * (count * (lats // 2)),
            [x, swap(x, "lat", 1), weights],
            8 * weights.shape[0] * x.size,
        )
        pieces = []
        for n in range(count):
            piece = out[n]
            for h in range(1, lats // 2):
                piece = piece + swap(out[h * count + n], "lat", 2 * h)
            pieces.append(piece)
        return pieces

    done = {}
    for k, piece in enumerate(lat_back(spread[0], early)):
        done[k] = swap(piece, "lon", k) if k > 0 else piece
    if early < lons:
        piece = swap(spread[1], "lon", early)
        [done[early]] = lat_back(piece, 1)
    arrived = {}
    for k in done:
        arrived[k, 0] = done[k]
        for q in range(1, slots):
            arrived[k, q] = swap(done[k], "tm", q)
    pieces = [arrived[k, q] for q in range(slots) for k in range(lons)]
    [result] = vmem_call(
        functools.partial(finish_kernel, lons, slots, share, group),
        [struct(*split_up)],
        [by_group, *pieces],
        control.size,
    )
    return result.reshape(control.shape)


def solution(mesh):
    placed = (
        P(None, None, "lat", "lon"),
        P("tm", None, None, "lat", "lon"),
        P(),
        P(),
        P("lat", None),
        P("lon", None),
        P("tm", None, "lat", "lon", None),
        P("tm", None, "lat", "lon"),
        P("tm", None, "lat", "lon", None),
        P("tm", None, "lat", "lon", None),
    )
    return jax.shard_map(
        per_device,
        mesh=mesh,
        in_specs=placed,
        out_specs=P(None, None, "lat", "lon"),
        check_vma=False,
    )
```

```python
import functools
import math

import jax
import jax.numpy as jnp
from jax import lax
from jax.experimental import pallas as pl
from jax.experimental.pallas import tpu as pltpu
from jax.sharding import PartitionSpec as P


HIGHEST = lax.Precision.HIGHEST
F32 = jnp.float32
BF16 = jnp.bfloat16


def swap(x, axis, k):
    return lax.ppermute(x, axis, [(i, i ^ k) for i in range(lax.axis_size(axis))])


def split(x):
    high = x.astype(BF16)
    return high, (x - high.astype(F32)).astype(BF16)


def dot(x, y, dims=((1,), (0,)), precision=None):
    return lax.dot_general(
        x, y, (dims, ((), ())), precision=precision, preferred_element_type=F32
    )


def vmem_call(kernel, out_shape, operands, flops, scratch=(), smem=0):
    specs = [pl.BlockSpec(memory_space=pltpu.SMEM)] * smem
    specs += [pl.BlockSpec(memory_space=pltpu.VMEM)] * (len(operands) - smem)
    nbytes = sum(math.prod(x.shape) * x.dtype.itemsize for x in [*operands, *out_shape])
    return pl.pallas_call(
        kernel,
        out_shape=out_shape,
        in_specs=specs,
        out_specs=[pl.BlockSpec(memory_space=pltpu.VMEM)] * len(out_shape),
        scratch_shapes=list(scratch),
        cost_estimate=pl.CostEstimate(flops=flops, bytes_accessed=nbytes, transcendentals=0),
        compiler_params=pltpu.CompilerParams(vmem_limit_bytes=2 * nbytes + 2**22),
    )(*operands)


def struct(*shape):
    return jax.ShapeDtypeStruct(shape, F32)


def cut_kernel(bands, slots, share, group, *refs):
    pert, outs, first, last = refs[0], refs[1:-2], refs[-2], refs[-1]
    rows, width = pert.shape[4:]
    t, b = lax.axis_index("tm"), lax.axis_index("lon")
    held = pert.shape[2]
    for q in range(slots):
        member = lax.div(t ^ q, held) * share
        level = lax.rem(t ^ q, held)
        for k in range(bands):
            for inner in range(group):
                part = pert[pl.ds(member, share), b ^ k, level, inner]
                part = part.astype(F32)
                at = inner * share * rows
                outs[q * bands + k][at : at + share * rows, :] = part.reshape(share * rows, width)
                at = ((q * bands + k) * group + inner) * share
                first[at : at + share, :] = part[:, 0, :]
                last[at : at + share, :] = part[:, rows - 1, :]


def weight_kernel(lats, rows, repeat, matrix, ahead, back):
    a = lax.axis_index("lat")
    length = matrix.shape[1]
    size = repeat * rows
    full = size + 2 * repeat
    iota = lax.broadcasted_iota

    def pick(shape, axis, wanted):
        return jnp.where(iota(jnp.int32, shape, axis) == wanted, 1.0, 0.0).astype(BF16)

    def block(to, of):
        line = iota(jnp.int32, (full, length), 0)
        rim = line - size
        wanted = jnp.where(
            rim < 0,
            to * rows + jnp.bitwise_and(line, rows - 1),
            to * rows + jnp.where(rim < repeat, -1, rows),
        )
        chosen = dot(pick((full, length), 1, wanted), matrix[...]).astype(BF16)
        column = iota(jnp.int32, (length, size), 1)
        chosen = dot(chosen, pick((length, size), 0, of * rows + jnp.bitwise_and(column, rows - 1)))
        line, column = iota(jnp.int32, (full, size), 0), iota(jnp.int32, (full, size), 1)
        rim = line - size
        field = jnp.where(rim < 0, line // rows, jnp.bitwise_and(rim, repeat - 1))
        return jnp.where(field == column // rows, chosen, 0.0)

    for h in range(0, lats, 2):
        at = h // 2 * full
        wide = jnp.concatenate([block(a ^ h, a ^ j) for j in (0, 1)], axis=1)
        ahead[at : at + full, :] = jnp.concatenate([wide, wide], axis=1).astype(BF16)
        at = h // 2 * size
        wide = jnp.concatenate([block(a ^ j, a ^ h).T for j in (0, 1)], axis=1)
        back[at : at + size, :] = jnp.concatenate([wide, wide], axis=1).astype(BF16)


def package_kernel(slots, count, cell, value, weight, *outs):
    t = lax.axis_index("tm")
    cap = cell.shape[1]
    entry = lax.broadcasted_iota(jnp.int32, (1, cap), 1)
    for q in range(slots):
        slot = t ^ q
        at = pl.ds(slot, 1)
        usable = jnp.where(entry < count[slot], 1.0, 0.0)
        lines = [cell[at, :].astype(F32), value[at, :], weight[at, :] * usable]
        outs[q][...] = jnp.concatenate(lines + [jnp.zeros((5, cap), F32)], axis=0)


def list_kernel(slots, held, half, *refs):
    package, interp, outs, turned = refs[:slots], refs[slots], refs[slots + 1 : -1], refs[-1]
    count, cap = interp.shape[0], package[0].shape[1]
    cols = interp.shape[1] // held
    part = lax.rem(lax.axis_index("tm"), held)
    mine = interp[:, :cols]
    for n in range(1, held):
        mine = jnp.where(part == n, interp[:, n * cols : (n + 1) * cols], mine)
    turned[...] = jnp.concatenate(
        [
            mine[1 : count - 1],
            mine[:1],
            mine[count - 1 :],
            jnp.zeros((turned.shape[0] - count, cols), F32),
        ],
        axis=0,
    )
    start = jnp.bitwise_and(lax.axis_index("lat"), 1) * (turned.shape[0] - half)
    outs[0][:half, :] = turned[pl.ds(pl.multiple_of(start, 8), half), :]
    at = outs[-1].shape[0] - 8
    for h in range(slots):
        outs[-1][at:, h * cap : (h + 1) * cap] = package[h][...]


def merge_kernel(bands, fields, *refs):
    rims, parts, outs = refs[:fields], refs[fields:-bands], refs[-bands:]
    edge = rims[0].shape[1]
    tall = outs[0].shape[0] - len(rims) * edge
    b = lax.axis_index("lon")
    for k in range(bands):
        at = pl.ds(pl.multiple_of((b ^ k) * tall, 8), tall)
        total = parts[0][at, :]
        for part in parts[1:]:
            total = total + part[at, :]
        outs[k][:tall, :] = total
        for q, rim in enumerate(rims):
            outs[k][tall + q * edge : tall + (q + 1) * edge, :] = rim[k]


def gather_kernel(*refs):
    out = refs[-1]
    for k, ref in enumerate(refs[:-1]):
        out[k] = ref[: out.shape[1], :]


def finish_kernel(bands, slots, share, group, control, *refs):
    pieces, out = refs[:-1], refs[-1]
    rows, width = control.shape[4:]
    t, b = lax.axis_index("tm"), lax.axis_index("lon")
    held = control.shape[2]
    for q in range(slots):
        member = pl.ds(lax.div(t ^ q, held) * share, share)
        level = lax.rem(t ^ q, held)
        for k in range(bands):
            for inner in range(group):
                at = inner * share * rows
                part = pieces[q * bands + k][at : at + share * rows, :].reshape(share, rows, width)
                old = control[member, b ^ k, level, inner]
                out[member, b ^ k, level, inner] = old + part


def spin_kernel(bands, matrix, table, turned):
    b = lax.axis_index("lon")
    width = matrix.shape[0] // bands
    for k in range(bands):
        at = pl.ds(pl.multiple_of((b ^ k) * width, width), width)
        for j in range(bands):
            block = matrix[at, pl.ds(pl.multiple_of((b ^ j) * width, width), width)]
            ks, js = slice(k * width, (k + 1) * width), slice(j * width, (j + 1) * width)
            table[ks, js] = block
            turned[js, ks] = block.astype(F32).T.astype(BF16)


def pairs(blocks):
    return [
        blocks[i] if i + 1 == len(blocks) else jnp.concatenate(blocks[i : i + 2], axis=1)
        for i in range(0, len(blocks), 2)
    ]


def lat_kernel(share, group, rows, repeat, own, other, weights, *outs):
    table = weights[...]
    size, width = repeat * rows, own.shape[1]
    full = size + 2 * repeat
    fields = group * share * rows
    tall = fields + 2 * group * share
    blocks = []
    for i in range(own.shape[0] // size):
        block = jnp.concatenate([ref[i * size : (i + 1) * size, :] for ref in (own, other)], axis=0)
        blocks.append(block)
    for pair, block in enumerate(pairs(blocks)):
        result = dot(table, jnp.concatenate(split(block), axis=0))
        for side in range(block.shape[1] // width):
            line = (2 * pair + side) * repeat
            band, inner, member = line // (group * share), line // share % group, line % share
            at = band * tall + (inner * share + member) * rows
            span = slice(side * width, (side + 1) * width)
            for h, out in enumerate(outs):
                base = h * full
                out[at : at + size, :] = result[base : base + size, span]
                for rim in (0, 1):
                    to = band * tall + fields + (2 * inner + rim) * share + member
                    of = base + size + rim * repeat
                    out[to : to + repeat, :] = result[of : of + repeat, span]


def lat_back_kernel(bands, share, group, rows, repeat, own, other, weights, *outs):
    table = weights[...]
    size, width = repeat * rows, own.shape[1]
    fields = group * share * rows
    tall = fields + 2 * group * share
    blocks, where = [], []
    for k in range(bands):
        for inner in range(group):
            for member in range(0, share, repeat):
                block = []
                for ref in (own, other):
                    at = k * tall + (inner * share + member) * rows
                    block.append(ref[at : at + size, :])
                    for rim in (0, 1):
                        at = k * tall + fields + (2 * inner + rim) * share + member
                        block.append(ref[at : at + repeat, :])
                blocks.append(jnp.concatenate(block, axis=0))
                where.append((k, (inner * share + member) * rows))
    for pair, block in enumerate(pairs(blocks)):
        result = dot(table, jnp.concatenate(split(block), axis=0))
        for side in range(block.shape[1] // width):
            k, at = where[2 * pair + side]
            span = slice(side * width, (side + 1) * width)
            for h in range(len(outs) // bands):
                outs[h * bands + k][at : at + size, :] = result[h * size : (h + 1) * size, span]


def increment_stage(sizes, source, table, pert, rims, window):
    bands, slots, share, group, rows, padded, width = sizes
    fields = group * share * rows
    pieces = [split(f[: fields + 2 * group * share, :]) for f in source]
    high, low = (jnp.concatenate([p[i] for p in pieces], axis=1) for i in (0, 1))
    part = table[...]
    spread = dot(high, part) + dot(low, part)
    filler = jnp.zeros((padded - rows - 2, width), F32)
    for q in range(slots):
        for k in range(bands):
            span = slice(k * width, (k + 1) * width)
            for inner in range(group):
                total = None
                for m in range(share):
                    at = (inner * share + m) * rows
                    term = spread[at : at + rows, span] * pert[q * bands + k][at : at + rows, :]
                    total = term if total is None else total + term
                block = [total]
                for rim in (0, 1):
                    at = (2 * inner + rim) * share
                    at_edge = rims[k].shape[0] + (q - slots) * 2 * group * share + at
                    edge = rims[k][at_edge : at_edge + share, :]
                    edge = spread[fields + at : fields + at + share, span] * edge
                    block.append(jnp.sum(edge, axis=0, keepdims=True))
                at = (q * group + inner) * padded
                window[k, at : at + padded, :] = jnp.concatenate(block + [filler], axis=0)


def observe_stage(sizes, window, tables, grad):
    bands, _, _, _, _, _, width = sizes
    onto, back, chosen, ends = tables
    tall = chosen.shape[1]
    lane = lax.broadcasted_iota(jnp.int32, (tall, width), 1)
    b = lax.axis_index("lon")
    for k in range(bands):
        grad[k] = jnp.zeros((tall, width), F32)
    for k in range(bands):
        before = b ^ lax.rem((b ^ k) + bands - 1, bands)
        after = b ^ lax.rem((b ^ k) + 1, bands)
        upper, lower = split(window[k])
        table = onto[k]
        left, right = ends[k, 0:1], ends[k, 1:2]
        seen_by = dot(jnp.concatenate([upper, upper], axis=1), table) + dot(lower, table[:width])
        seen_by += window[before][:, width - 1 : width] * left
        seen_by += window[after][:, 0:1] * right
        pick = chosen[k]
        seen = jnp.sum(pick * seen_by, axis=0, keepdims=True)
        weighted = pick * (ends[k, 4:5] * (seen - ends[k, 3:4]))
        upper, lower = split(weighted)
        table = back[k]
        both = dot(upper, table)
        grad[k] += both[:, :width] + both[:, width:] + dot(lower, table[:, :width])
        onto_left = jnp.sum(weighted * left, axis=1, keepdims=True)
        onto_right = jnp.sum(weighted * right, axis=1, keepdims=True)
        grad[before] += jnp.where(lane == width - 1, onto_left, 0.0)
        grad[after] += jnp.where(lane == 0, onto_right, 0.0)


def adjoint_stage(sizes, grads, table, pert, rims, outs):
    bands, slots, share, group, rows, padded, width = sizes
    held = slots // len(grads)
    fields = group * share * rows
    columns = []
    for k in range(bands):
        pieces = []
        for inner in range(group):
            lines = [
                grads[q // held][k, pl.ds((q % held * group + inner) * padded, padded), :]
                for q in range(slots)
            ]
            for m in range(share):
                at = (inner * share + m) * rows
                pieces.append(sum(
                    lines[q][:rows] * pert[q * bands + k][at : at + rows, :] for q in range(slots)
                ))
        for inner in range(group):
            for rim in (0, 1):
                at = (2 * inner + rim) * share
                total = 0.0
                for q in range(slots):
                    line = (q % held * group + inner) * padded + rows + rim
                    line = grads[q // held][k, line : line + 1, :]
                    edge = rims[k].shape[0] + (q - slots) * 2 * group * share + at
                    total += line * rims[k][edge : edge + share, :]
                pieces.append(total)
        columns.append(split(jnp.concatenate(pieces, axis=0)))
    high, low = (jnp.concatenate([c[i] for c in columns], axis=1) for i in (0, 1))
    part = table[...]
    result = dot(high, part) + dot(low, part)
    tall = fields + 2 * group * share
    for k in range(bands):
        out, at = (outs[1 + k // 2], 0) if k % 2 else (outs[0], k // 2 * tall)
        out[at : at + tall, :] = result[:, k * width : (k + 1) * width]


def middle_kernel(sizes, *refs):
    bands, slots = sizes[:2]
    source, turned, table, rest = refs[:bands], refs[bands], refs[bands + 1], refs[bands + 2 :]
    pert, rims, rest = rest[: slots * bands], source, rest[slots * bands :]
    tables, outs, (window, grad) = rest[:4], rest[4:-2], rest[-2:]
    increment_stage(sizes, source, turned, pert, rims, window)
    observe_stage(sizes, window, tables, grad)
    adjoint_stage(sizes, [grad], table, pert, rims, outs)


def increment_kernel(sizes, *refs):
    bands = sizes[0]
    pert, out = refs[bands + 1 : -1], refs[-1]
    increment_stage(sizes, refs[:bands], refs[bands], pert, refs[:bands], out)


def observe_kernel(sizes, window, onto, back, chosen, ends, grad):
    observe_stage(sizes, window, (onto, back, chosen, ends), grad)


def adjoint_kernel(sizes, sets, *refs):
    bands, slots = sizes[:2]
    grads, table, rest = refs[:sets], refs[sets], refs[sets + 1 :]
    pert, rest = rest[: bands * slots], rest[bands * slots :]
    adjoint_stage(sizes, grads, table, pert, rest[:bands], rest[bands:])


def prepare_kernel(sizes, held, half, fine, *refs):
    bands, _, _, levels, rows, padded, width = sizes
    parts, packs, interp_lat = refs[: 2 * held], refs[2 * held : 3 * held], refs[3 * held]
    onto, back, chosen, ends, full = refs[3 * held + 1 :]
    fine_rows, fine_cols = fine
    count = packs[0].shape[2]
    obs = held * count
    cols = fine_cols // held
    tm = lax.rem(lax.axis_index("tm"), held)
    first = ((lax.axis_index("lon") * held + tm) * levels).astype(F32)
    parity = jnp.bitwise_and(lax.axis_index("lat"), 1)
    lat = interp_lat[...]
    lat = jnp.concatenate(
        [lat[1 : rows + 1], lat[:1], lat[rows + 1 :], jnp.zeros((padded - rows - 2, fine_rows), F32)], axis=0
    )
    slot = lax.broadcasted_iota(jnp.int32, (1, obs), 1) // count
    for k in range(bands):
        base = packs[0].shape[1] - 8
        lines = jnp.concatenate([pack[k, base:, :] for pack in packs], axis=1)
        cell = lines[0:1] + 0.5
        level = jnp.floor(cell * (1.0 / (fine_rows * fine_cols)))
        inside = cell - level * (fine_rows * fine_cols)
        row = jnp.floor(inside * (1.0 / fine_cols))
        col = jnp.floor(inside - row * fine_cols).astype(jnp.int32)
        line = lax.broadcasted_iota(jnp.int32, (cols, obs), 0)
        hot = [
            jnp.where(line == col - jnp.bitwise_xor(tm, j) * cols, 1.0, 0.0).astype(BF16)
            for j in range(held)
        ]
        hot = jnp.concatenate(hot, axis=0)
        for side in (0, 1):
            part = jnp.concatenate([parts[2 * j + side][k, :half, :] for j in range(held)], axis=1)
            upper, lower = split(part)
            start = jnp.bitwise_xor(parity, side) * (full.shape[0] - half)
            full[pl.ds(pl.multiple_of(start, 8), half), :] = dot(upper, hot) + dot(lower, hot)
        main = full[:width, :]
        upper, lower = split(main)
        onto[k, :width, :] = upper
        onto[k, width:, :] = lower
        upper, lower = split(main.T)
        back[k, :, :width] = upper
        back[k, :, width:] = lower
        line = lax.broadcasted_iota(jnp.int32, (fine_rows, obs), 0)
        hot = jnp.where(line == row.astype(jnp.int32), 1.0, 0.0)
        rowpart = dot(lat, hot, precision=HIGHEST)
        ends[k] = jnp.concatenate([full[width : width + 2, :], level, lines[1:3], lines[3:6]], axis=0)
        for j in range(held):
            for inner in range(levels):
                at = (j * levels + inner) * padded
                fits = jnp.logical_and(level == first + inner, slot == j)
                chosen[k, at : at + padded, :] = jnp.where(fits, rowpart, 0.0)


def per_device(
    control,
    ens_pert,
    lat_filter,
    lon_filter,
    interp_lat,
    interp_lon,
    obs_cell,
    obs_count,
    obs_value,
    obs_weight,
):
    slots, lats, lons = (lax.axis_size(axis) for axis in ("tm", "lat", "lon"))
    t, a, _ = (lax.axis_index(axis) for axis in ("tm", "lat", "lon"))
    members, levels, rows, width = control.shape
    held = math.gcd(slots, levels // lons)
    parts = slots // held
    share = members // parts
    group = levels // (lons * held)
    fields = group * share * rows
    edge = 2 * group * share
    tall = fields + edge
    whole = lons * width
    padded = -(-(rows + 2) // 8) * 8
    sizes = (lons, slots, share, group, rows, padded, width)
    split_up = (members, lons, held, group, rows, width)
    by_group = control.reshape(split_up)

    repeat = math.gcd(share, max(64 // rows, 1))

    size = repeat * rows
    full = size + 2 * repeat
    ahead, weights = vmem_call(
        functools.partial(weight_kernel, lats, rows, repeat),
        [
            jax.ShapeDtypeStruct((lats // 2 * full, 4 * size), BF16),
            jax.ShapeDtypeStruct((lats // 2 * size, 4 * full), BF16),
        ],
        [lat_filter],
        0,
    )

    count = slots * lons
    cut = vmem_call(
        functools.partial(cut_kernel, lons, slots, share, group),
        [struct(fields, width)] * count + [struct(count * group * share, width)] * 2,
        [ens_pert[0].reshape(split_up)],
        0,
    )
    pert = [None] * count
    order = [*range(2, lons), *range(1, min(lons, 2)), 0]
    for k in order:
        for q in range(slots):
            piece = cut[q * lons + k]
            if q > 0:
                piece = swap(piece, "tm", q)
            pert[q * lons + k] = piece if k == 0 else swap(piece, "lon", k)
    mine = lax.dynamic_slice(
        by_group,
        (t // held * share, 0, t % held, 0, 0, 0),
        (share, lons, 1, group, rows, width),
    )
    mine = jnp.transpose(mine, (1, 2, 3, 0, 4, 5)).reshape(lons * fields, width)
    mixed = vmem_call(
        functools.partial(lat_kernel, share, group, rows, repeat),
        [struct(lons * tall, width)] * (lats // 2),
        [mine, swap(mine, "lat", 1), ahead],
        2 * ahead.shape[0] * 4 * mine.size,
    )
    arrived = [swap(mixed[h], "lat", 2 * h) for h in range(1, lats // 2)]

    rim = cut[-2:]
    odd = jnp.bitwise_and(a, 1) == 1
    inside = swap(jnp.where(odd, rim[0], rim[1]), "lat", 1)
    across = [(i, i + 1) for i in range(1, lats - 1, 2)]
    across += [(j, i) for i, j in across]
    outside = lax.ppermute(jnp.where(odd, rim[1], rim[0]), "lat", across)
    form = (slots, lons, group, 1, share, width)
    before = jnp.where(odd, inside, outside).reshape(form)
    after = jnp.where(odd, outside, inside).reshape(form)
    rim = jnp.concatenate([before, after], axis=3).reshape(slots, lons, edge, width)
    rims = [rim[0]] + [swap(rim[q], "tm", q) for q in range(1, slots)]

    cap = obs_cell.shape[-1]
    package = vmem_call(
        functools.partial(package_kernel, slots),
        [struct(8, cap)] * slots,
        [obs_count.reshape(slots)] + [x.reshape(slots, cap) for x in (obs_cell, obs_value, obs_weight)],
        0,
        smem=1,
    )
    package = [package[0]] + [swap(package[q], "tm", q) for q in range(1, slots)]
    entries = slots * cap
    fine = interp_lat.shape[0], interp_lon.shape[0]
    cols = fine[1] // held
    turned_rows = -(-(width + 2) // 8) * 8
    half = -(-turned_rows // 16) * 8
    fuse = entries == cols
    shapes = [struct(half + 8, cols)] if fuse else [struct(half, cols), struct(8, entries)]
    listing = vmem_call(
        functools.partial(list_kernel, slots, held, half),
        shapes,
        [*package, interp_lon.T],
        0,
        scratch=[pltpu.VMEM((turned_rows, cols), F32)],
    )
    near = [[x] + [swap(x, "lon", k) for k in range(1, lons)] for x in listing]
    source = vmem_call(
        functools.partial(merge_kernel, lons, slots),
        [struct(tall + slots * edge, width)] * lons,
        [*rims, mixed[0], *arrived],
        0,
    )
    source = [source[0]] + [swap(source[k], "lon", k) for k in range(1, lons)]
    near = [vmem_call(gather_kernel, [struct(lons, *x[0].shape)], x, 0)[0] for x in near]
    slices, packs = [], []
    for j in range(held):
        here = near if j == 0 else [swap(x, "tm", j) for x in near]
        slices += [here[0], swap(here[0], "lat", 1)]
        packs.append(here[-1])
    window_rows = held * group * padded
    obs = held * entries
    lists = vmem_call(
        functools.partial(prepare_kernel, sizes, held, half, fine),
        [
            jax.ShapeDtypeStruct((lons, 2 * width, obs), BF16),
            jax.ShapeDtypeStruct((lons, obs, 2 * width), BF16),
            struct(lons, window_rows, obs),
            struct(lons, 8, obs),
        ],
        [*slices, *packs, interp_lat.T],
        8 * lons * obs * width * fine[1],
        scratch=[pltpu.VMEM((turned_rows, obs), F32)],
    )

    table, turned = vmem_call(
        functools.partial(spin_kernel, lons),
        [jax.ShapeDtypeStruct((whole, whole), BF16)] * 2,
        [lon_filter],
        0,
    )
    flops = 4 * tall * whole * whole
    scratch = [pltpu.VMEM((lons, window_rows, width), F32)] * 2
    early = (lons + 1) // 2
    shapes = [struct(early * tall, width)] + [struct(tall, width)] * (lons - early)
    if parts == 1:
        spread = vmem_call(
            functools.partial(middle_kernel, sizes),
            shapes,
            [*source, turned, table, *pert, *lists],
            2 * flops,
            scratch=scratch,
        )
    else:
        [every] = vmem_call(
            functools.partial(increment_kernel, sizes),
            [struct(lons, slots * group * padded, width)],
            [*source, turned, *pert],
            flops,
        )
        window = every[:, :window_rows]
        for h in range(1, parts):
            window += swap(every[:, h * window_rows :][:, :window_rows], "tm", h * held)
        [grad] = vmem_call(
            functools.partial(observe_kernel, sizes),
            [struct(lons, window_rows, width)],
            [window, *lists],
            8 * window_rows * whole * obs,
        )
        grads = [grad] + [swap(grad, "tm", h * held) for h in range(1, parts)]
        spread = vmem_call(
            functools.partial(adjoint_kernel, sizes, parts),
            shapes,
            [*grads, table, *pert, *source],
            flops,
        )

    def lat_back(x, count):
        out = vmem_call(
            functools.partial(lat_back_kernel, count, share, group, rows, repeat),
            [struct(fields, width)] * (count * (lats // 2)),
            [x, swap(x, "lat", 1), weights],
            8 * weights.shape[0] * x.size,
        )
        pieces = []
        for n in range(count):
            piece = out[n]
            for h in range(1, lats // 2):
                piece = piece + swap(out[h * count + n], "lat", 2 * h)
            pieces.append(piece)
        return pieces

    done = {}
    for n, piece in enumerate(lat_back(spread[0], early)):
        done[2 * n] = swap(piece, "lon", 2 * n) if n > 0 else piece
    for k in range(1, lons, 2):
        piece = swap(spread[1 + k // 2], "lon", k)
        [done[k]] = lat_back(piece, 1)
    arrived = {}
    for k in done:
        arrived[k, 0] = done[k]
        for q in range(1, slots):
            arrived[k, q] = swap(done[k], "tm", q)
    pieces = [arrived[k, q] for q in range(slots) for k in range(lons)]
    [result] = vmem_call(
        functools.partial(finish_kernel, lons, slots, share, group),
        [struct(*split_up)],
        [by_group, *pieces],
        control.size,
    )
    return result.reshape(control.shape)


def solution(mesh):
    placed = (
        P(None, None, "lat", "lon"),
        P("tm", None, None, "lat", "lon"),
        P(),
        P(),
        P("lat", None),
        P("lon", None),
        P("tm", None, "lat", "lon", None),
        P("tm", None, "lat", "lon"),
        P("tm", None, "lat", "lon", None),
        P("tm", None, "lat", "lon", None),
    )
    return jax.shard_map(
        per_device,
        mesh=mesh,
        in_specs=placed,
        out_specs=P(None, None, "lat", "lon"),
        check_vma=False,
    )
```
